256 devices in a mesh: section: 2 (over core), req: 16 (over x, y), head: 8 (over z).
Axes of the slice: x: 4, y: 4, z: 8, core: 2. Of those that a mesh axis runs over, the one named last changes fastest.
Arguments:
- tokens: bfloat16 [256, 8192], P(None, 'req'), may hold values from -14 to 14
- attention_gain: bfloat16 [2, 8192], P('section', 'req'), may hold values from 0.099609375 to 1.8984375
- query_key_value_weight: bfloat16 [2, 8192, 8, 1280], P('section', 'req', 'head'), may hold values from -0.0625 to 0.0625
- head_output_weight: bfloat16 [2, 8, 1024, 8192], P('section', 'head', None, 'req'), may hold values from -0.0625 to 0.0625
- feedforward_gain: bfloat16 [2, 8192], P('section', 'req'), may hold values from 0.099609375 to 1.8984375
- gate_up: bfloat16 [2, 8192, 2, 14336], P('section', 'req', None, 'head'), may hold values from -0.0625 to 0.0625
- down_weight: bfloat16 [2, 14336, 8192], P('section', 'head', 'req'), may hold values from -0.046875 to 0.046875
- packed_cache: bfloat16 [2, 32768, 8, 256], P('section', 'req', 'head'), may hold values from -70 to 70
- long_cache: bfloat16 [2, 2, 32768, 8, 256], P('section', None, 'req', 'head'), may hold values from -70 to 70
- lengths: int32 [16, 16], P('req'), may hold values from 1 to 256, 2048 in all within a row
- long_split: int32 [2, 16], P(None, 'req'), may hold values from 1 to 2048, 16384 in all within a row
Outputs:
- layer_outputs: bfloat16 [2, 256, 8192], P('section', None, 'req')
The draws below stay inside these ranges and needn't reach their ends.
Inputs may be any that keep to these rules, and one draw needn't show every extreme that they name: Row g holds the lengths of the 16 requests of request group g in order; they sum to 2048, and the requests' keys fill that group's 2048 slots of packed_cache one request after another. `long_split`: entry (j, g) counts the live slots, the first ones, of group g's 2048 slots of long request j; each row sums to 16384.
All inputs are finite; a program needn't handle non-finite values.
Results may differ from the reference program's by a relative error of at most 0.04.
Values may be sent and summed in bfloat16 or wider, within the bound.
A program may use at most 64 MiB of HBM per device.

```python
import math
import jax
import jax.numpy as jnp
import numpy as np
from jax import lax

MODEL_WIDTH = 8192
QUERY_HEADS = 64
KEY_VALUE_HEADS = 8
HEAD_SIZE = 128
FF = 14336
GROUP_REQUESTS = 16
LONG = 16384
GROUP_SLOTS = 2048
LONG_GROUP_SLOTS = 2048
REQUEST_COUNT = 256
N_REQ = 16


def cached_value_rows(key, shape):
    base = jnp.clip(jax.random.normal(key, shape, jnp.float32), -6.0, 6.0)
    values = jnp.concatenate([2.0 * base[..., :HEAD_SIZE], 3.0 * base[..., HEAD_SIZE:]], -1)
    return values.astype(jnp.bfloat16)


def draw_packed_cache(key, part):
    return cached_value_rows(jax.random.fold_in(key, 101), (2, N_REQ * GROUP_SLOTS, KEY_VALUE_HEADS, 2 * HEAD_SIZE))


def draw_long_cache(key, part):
    return cached_value_rows(jax.random.fold_in(key, 202), (2, 2, N_REQ * LONG_GROUP_SLOTS, KEY_VALUE_HEADS, 2 * HEAD_SIZE))


def draw_tokens(key, part):
    shape = (REQUEST_COUNT, MODEL_WIDTH)
    fraction = jnp.arange(MODEL_WIDTH).astype(jnp.float32) / (MODEL_WIDTH - 1)
    column_scale = jnp.exp(jnp.log(0.4) + fraction * jnp.log(5.0))
    base = jnp.clip(jax.random.normal(jax.random.fold_in(key, 303), shape, jnp.float32), -6.0, 6.0)
    return (base * column_scale[None, :]).astype(jnp.bfloat16)


def block_levels(own_key, shape, pieces, smallest, largest):
    gain = 1.0
    for dim, parts in pieces:
        steps = jax.random.uniform(jax.random.fold_in(jax.random.fold_in(own_key, 6), dim), (parts,), jnp.float32, smallest / len(pieces), largest / len(pieces))
        gain = gain * jnp.repeat(jnp.exp(steps), shape[dim] // parts).reshape((-1,) + (1,) * (len(shape) - 1 - dim))
    return gain


def profile(count, total, bound, slope):
    loads = [(1 << 20) // math.isqrt(standing ** slope) + 1 for standing in range(2, count + 1)]
    surplus, counts = total - bound - (count - 1), [1] * (count - 1)
    while surplus > 0:
        candidates = [i for i in range(count - 1) if counts[i] < bound]
        mass, remaining = sum([loads[i] for i in candidates]), surplus
        for i in candidates:
            addition = min(bound - counts[i], max(1, remaining * loads[i] // mass), surplus)
            counts[i] = counts[i] + addition
            surplus = surplus - addition
    return np.array([bound] + counts)


def ragged_sizes(stream_key, count, total, most, lean):
    if count == 2:
        one = jax.random.randint(stream_key, (), max(1, total - most), min(most, total - 1) + 1)
        return jnp.stack([one, total - one])
    sizes = jnp.asarray(profile(count, total, most, lean), jnp.int32)
    pairs = (count - 1) // 2
    source_of, sink = sizes[1:1 + 2 * pairs:2], sizes[2:2 + 2 * pairs:2]
    margin = jnp.minimum(source_of - 1, most - sink)
    shifted = jax.random.randint(jax.random.fold_in(stream_key, 1), (pairs,), 0, 1 << 20) % (margin + 1)
    sizes = sizes.at[1:1 + 2 * pairs:2].set(source_of - shifted).at[2:2 + 2 * pairs:2].set(sink + shifted)
    return sizes[jax.random.permutation(jax.random.fold_in(stream_key, 2), count)]


def centred(own_key, shape, scale, most, pieces=(), dtype=jnp.bfloat16):
    array = jax.random.normal(own_key, shape, jnp.float32) * scale
    if len(pieces) > 0:
        array = block_levels(own_key, shape, pieces, -0.22, 0.18) * array
    return jnp.clip(array, min=-most, max=most).astype(dtype)


def setup_inputs(seed: int = 0) -> dict:
    key_of = jax.random.split(jax.random.key(seed), 12)
    tokens = draw_tokens(jax.random.fold_in(key_of[11], 71), 0)
    attention_gain = jnp.clip(1.0 + 0.18 * jax.random.normal(key_of[1], (2, MODEL_WIDTH), jnp.float32), 0.099609375, 1.8984375).astype(jnp.bfloat16)
    query_key_value_weight = centred(key_of[2], (2, MODEL_WIDTH, KEY_VALUE_HEADS, (QUERY_HEADS // KEY_VALUE_HEADS + 2) * HEAD_SIZE), MODEL_WIDTH ** -0.5, 0.0625, ((0, 2), (1, 16), (2, 8)))
    head_output_weight = centred(key_of[3], (2, KEY_VALUE_HEADS, (QUERY_HEADS // KEY_VALUE_HEADS) * HEAD_SIZE, MODEL_WIDTH), (QUERY_HEADS * HEAD_SIZE) ** -0.5, 0.0625, ((0, 2), (1, 8), (3, 16)))
    feedforward_gain = jnp.clip(1.0 + 0.18 * jax.random.normal(key_of[4], (2, MODEL_WIDTH), jnp.float32), 0.099609375, 1.8984375).astype(jnp.bfloat16)
    gate_up = centred(key_of[5], (2, MODEL_WIDTH, 2, FF), MODEL_WIDTH ** -0.5, 0.0625, ((0, 2), (1, 16), (3, 8)))
    down_weight = centred(key_of[6], (2, FF, MODEL_WIDTH), FF ** -0.5, 0.046875, ((0, 2), (1, 8), (2, 16)))
    packed_cache = draw_packed_cache(jax.random.fold_in(key_of[11], 71), 0)
    long_cache = draw_long_cache(jax.random.fold_in(key_of[11], 71), 0)
    lengths = jax.vmap(lambda own: ragged_sizes(own, GROUP_REQUESTS, GROUP_SLOTS, 256, 2))(jax.random.split(key_of[9], N_REQ)).reshape((N_REQ, GROUP_REQUESTS)).astype(jnp.int32)
    long_split = jax.vmap(lambda own: ragged_sizes(own, N_REQ, LONG, LONG_GROUP_SLOTS, 1))(jax.random.split(key_of[10], 2)).reshape((2, N_REQ)).astype(jnp.int32)
    return dict(tokens=tokens, attention_gain=attention_gain, query_key_value_weight=query_key_value_weight, head_output_weight=head_output_weight, feedforward_gain=feedforward_gain, gate_up=gate_up, down_weight=down_weight, packed_cache=packed_cache, long_cache=long_cache, lengths=lengths, long_split=long_split)


EPSILON = 1e-05

def rotate(values, position):
    half_dim = values.shape[-1] // 2
    freq_ids = jnp.arange(half_dim).astype(jnp.float32)
    inverse = 1.0 / 10000.0 ** (freq_ids * 2.0 / values.shape[-1])
    angles = position.astype(jnp.float32)[:, None] * inverse[None, :]
    cosine = jnp.cos(angles)[:, None, None, :]
    sine_part = jnp.sin(angles)[:, None, None, :]
    lower_half = values[..., :half_dim]
    upper_half = values[..., half_dim:]
    return jnp.concatenate([lower_half * cosine - upper_half * sine_part, upper_half * cosine + lower_half * sine_part], -1)

def norm_rows(values, gain_row):
    floats = values.astype(jnp.float32)
    squares = lax.optimization_barrier(jnp.mean(floats * floats, axis=-1, keepdims=True))
    return (floats * lax.rsqrt(squares + EPSILON) * gain_row.astype(jnp.float32)).astype(jnp.bfloat16)

def decoder_layer(inputs, attention_gain, query_key_value_weight, head_output_weight, feedforward_gain, gate_up, down_weight, packed_cache, long_cache, lengths, long_split):
    requests_per_group = QUERY_HEADS // KEY_VALUE_HEADS
    score_scale = 1.0 / math.sqrt(HEAD_SIZE)
    normalized_input = norm_rows(inputs, attention_gain)
    projected_rows = jnp.dot(normalized_input, query_key_value_weight.reshape(MODEL_WIDTH, KEY_VALUE_HEADS * (requests_per_group + 2) * HEAD_SIZE), preferred_element_type=jnp.float32)
    projected_rows = projected_rows.reshape(REQUEST_COUNT, KEY_VALUE_HEADS, requests_per_group + 2, HEAD_SIZE)
    row_ids = jnp.arange(REQUEST_COUNT)
    long_row = (row_ids == 0) | (row_ids == N_REQ // 2 * GROUP_REQUESTS)
    position = lengths.reshape(REQUEST_COUNT) + jnp.where(long_row, LONG, 0).astype(jnp.int32)
    queries = rotate(projected_rows[:, :, :requests_per_group], position).astype(jnp.bfloat16)
    new_key = rotate(projected_rows[:, :, requests_per_group:requests_per_group + 1], position)[:, :, 0].astype(jnp.bfloat16)
    new_value = projected_rows[:, :, requests_per_group + 1].astype(jnp.bfloat16)
    far_keys = long_cache[..., :HEAD_SIZE].astype(jnp.float32)
    far_values = long_cache[..., HEAD_SIZE:].astype(jnp.float32)

    def attend(group_id):
        start_row = group_id * GROUP_REQUESTS
        group_queries = lax.dynamic_slice_in_dim(queries, start_row, GROUP_REQUESTS, 0).astype(jnp.float32)
        group_keys = lax.dynamic_slice_in_dim(new_key, start_row, GROUP_REQUESTS, 0).astype(jnp.float32)
        group_values = lax.dynamic_slice_in_dim(new_value, start_row, GROUP_REQUESTS, 0).astype(jnp.float32)
        group_lengths = lax.dynamic_index_in_dim(lengths, group_id, 0, keepdims=False)
        pack_part = lax.dynamic_slice_in_dim(packed_cache, group_id * GROUP_SLOTS, GROUP_SLOTS, 0).astype(jnp.float32)
        seg_ends = jnp.cumsum(group_lengths)
        slot_ids = jnp.arange(GROUP_SLOTS)
        slot_owner = lax.optimization_barrier(jnp.sum((slot_ids[:, None] >= seg_ends[None, :]).astype(jnp.int32), axis=1))
        in_segment = (slot_owner[None, :] == jnp.arange(GROUP_REQUESTS)[:, None])[:, None, None, :]
        scores = jnp.einsum('rkhd,pkd->rkhp', group_queries, pack_part[..., :HEAD_SIZE]) * score_scale
        own_score = jnp.einsum('rkhd,rkd->rkh', group_queries, group_keys) * score_scale
        long_id = jnp.where(group_id == 0, 0, 1)
        is_long = (group_id == 0) | (group_id == N_REQ // 2)
        split_row = lax.dynamic_index_in_dim(long_split, long_id, 0, keepdims=False)
        far_live = (jnp.arange(LONG_GROUP_SLOTS)[None, :] < split_row[:, None]).reshape(N_REQ * LONG_GROUP_SLOTS) & is_long
        far_key = lax.dynamic_index_in_dim(far_keys, long_id, 0, keepdims=False)
        far_value = lax.dynamic_index_in_dim(far_values, long_id, 0, keepdims=False)
        far_scores = jnp.einsum('khd,pkd->khp', group_queries[0], far_key) * score_scale
        far_live = far_live[None, None, :]
        row_max = jnp.maximum(lax.optimization_barrier(jnp.max(jnp.where(in_segment, scores, -jnp.inf), axis=-1)), own_score)
        far_max = lax.optimization_barrier(jnp.max(jnp.where(far_live, far_scores, -jnp.inf), axis=-1))
        row_max = row_max.at[0].set(jnp.maximum(row_max[0], far_max))
        weights = jnp.where(in_segment, jnp.exp(jnp.where(in_segment, scores - row_max[..., None], 0.0)), 0.0).astype(jnp.bfloat16)
        own_weights = jnp.exp(own_score - row_max).astype(jnp.bfloat16)
        far_weights = jnp.where(far_live, jnp.exp(jnp.where(far_live, far_scores - row_max[0][..., None], 0.0)), 0.0).astype(jnp.bfloat16)
        softmax_total = lax.optimization_barrier(jnp.sum(weights.astype(jnp.float32), axis=-1)) + own_weights.astype(jnp.float32)
        softmax_total = softmax_total.at[0].add(lax.optimization_barrier(jnp.sum(far_weights.astype(jnp.float32), axis=-1)))
        weighted_sum = jnp.einsum('rkhp,pkd->rkhd', weights.astype(jnp.float32), pack_part[..., HEAD_SIZE:])
        weighted_sum = weighted_sum + own_weights.astype(jnp.float32)[..., None] * group_values[:, :, None, :]
        weighted_sum = weighted_sum.at[0].add(jnp.einsum('khp,pkd->khd', far_weights.astype(jnp.float32), far_value))
        return (weighted_sum / softmax_total[..., None]).astype(jnp.bfloat16).reshape(GROUP_REQUESTS, KEY_VALUE_HEADS * requests_per_group * HEAD_SIZE)
    attended_heads = lax.map(attend, jnp.arange(N_REQ)).reshape(REQUEST_COUNT, QUERY_HEADS * HEAD_SIZE)
    attended = jnp.dot(attended_heads, head_output_weight.reshape(QUERY_HEADS * HEAD_SIZE, MODEL_WIDTH), preferred_element_type=jnp.float32)
    residual = (inputs.astype(jnp.float32) + attended).astype(jnp.bfloat16)
    normed_two = norm_rows(residual, feedforward_gain)
    gate_and_up = jnp.dot(normed_two, gate_up.reshape(MODEL_WIDTH, 2 * FF), preferred_element_type=jnp.float32)
    hidden = (jax.nn.silu(gate_and_up[:, :FF]) * gate_and_up[:, FF:]).astype(jnp.bfloat16)
    lowered = jnp.dot(hidden, down_weight, preferred_element_type=jnp.float32)
    return (residual.astype(jnp.float32) + lowered).astype(jnp.bfloat16)

def reference(tokens, attention_gain, query_key_value_weight, head_output_weight, feedforward_gain, gate_up, down_weight, packed_cache, long_cache, lengths, long_split):
    first_out = decoder_layer(tokens, attention_gain[0], query_key_value_weight[0], head_output_weight[0], feedforward_gain[0], gate_up[0], down_weight[0], packed_cache[0], long_cache[0], lengths, long_split)
    second_out = decoder_layer(first_out, attention_gain[1], query_key_value_weight[1], head_output_weight[1], feedforward_gain[1], gate_up[1], down_weight[1], packed_cache[1], long_cache[1], lengths, long_split)
    return jnp.stack([first_out, second_out])
```

```python
import functools
import math

import jax
import jax.numpy as jnp
from jax import lax
from jax.experimental import pallas as pl
from jax.experimental.pallas import tpu as pltpu
from jax.sharding import PartitionSpec as P

HEAD = 128
LONG = 16384
EPSILON = 1e-05
NEG = -1e30
F32 = jnp.float32
BF16 = jnp.bfloat16
MESH = pl.DeviceIdType.MESH


def split_two(value, lanes):
    high = value.astype(BF16).astype(F32)
    return jnp.where(lanes < 64, high, value - high).astype(BF16)


def rope(block, table):
    swapped = jnp.concatenate([block[:, HEAD // 2 :], block[:, : HEAD // 2]], axis=1)
    return block * table[:, :HEAD] + swapped * table[:, HEAD:]


def kernel(
    dims,
    split_ref,
    tok_ref,
    gain1_ref,
    wqkv_hbm,
    wo_hbm,
    gain2_ref,
    wgu_hbm,
    wd_hbm,
    pack_hbm,
    far_hbm,
    len_ref,
    cs_ref,
    out_ref,
    wqkv,
    wo,
    wgu,
    wd,
    pack,
    far,
    xin,
    xg,
    send1,
    recv1,
    ext32,
    exts,
    csl,
    qbuf,
    score,
    att,
    lse,
    fscore,
    rows_all,
    far_all,
    send3,
    recv3,
    res_all,
    send5,
    recv5,
    hid_all,
    send7,
    recv7,
    oblk,
    out_all,
    wsem,
    s1,
    r1,
    se,
    re,
    sc,
    rc,
    s2,
    r2,
    sl,
    rl,
    s3,
    r3,
    s4,
    r4,
    s5,
    r5,
    s6,
    r6,
    s7,
    r7,
    s8,
    r8,
    su,
    ru,
    sb,
    rb,
):
    n_req, n_head, width = dims
    n_y = 4 if n_req == 16 else n_req
    n_x = n_req // n_y
    sec = lax.axis_index("section")
    me = lax.axis_index("req")
    mz = lax.axis_index("head")
    blk, cols = xin.shape[1], xin.shape[2]
    rows = n_head * blk
    slots = pack.shape[0]
    heads = 8
    qw = heads * HEAD
    ff = wd.shape[0]
    scale = 1.0 / math.sqrt(HEAD)
    half = n_req // 2

    def req_peer(k):
        x = lax.rem(lax.div(me, n_y) + lax.div(k, n_y), n_x)
        y = lax.rem(lax.rem(me, n_y) + lax.rem(k, n_y), n_y)
        return x * n_y + y

    def head_peer(k):
        return lax.rem(mz + k, n_head)

    def req_copy(src, dst, ssem, rsem, peer):
        return pltpu.make_async_remote_copy(
            src_ref=src, dst_ref=dst, send_sem=ssem, recv_sem=rsem,
            device_id={"req": peer}, device_id_type=MESH,
        )

    def head_copy(src, dst, ssem, rsem, peer):
        return pltpu.make_async_remote_copy(
            src_ref=src, dst_ref=dst, send_sem=ssem, recv_sem=rsem,
            device_id={"head": peer}, device_id_type=MESH,
        )

    def spread(copy, count, peer_of, source, target, ssem, rsem, mine):
        @pl.loop(1, count)
        def _(k):
            peer = peer_of(k)
            copy(source(peer), target.at[mine], ssem.at[k], rsem.at[mine], peer).start()

    def arrived(copy, count, peer_of, target, ssem, rsem):
        @pl.loop(1, count)
        def _(k):
            peer = peer_of(k)
            copy(target.at[peer], target.at[peer], ssem.at[k], rsem.at[peer], peer).wait_recv()

    def sent(copy, count, peer_of, source, target, ssem, rsem, mine):
        @pl.loop(1, count)
        def _(k):
            peer = peer_of(k)
            copy(source(peer), target.at[mine], ssem.at[k], rsem.at[mine], peer).wait_send()

    loads = [
        pltpu.make_async_copy(src, dst, wsem.at[n])
        for n, (src, dst) in enumerate(
            ((wqkv_hbm, wqkv), (pack_hbm, pack), (far_hbm, far), (wo_hbm, wo), (wgu_hbm, wgu), (wd_hbm, wd))
        )
    ]
    for load in loads:
        load.start()

    barrier = pltpu.get_barrier_semaphore()

    @pl.loop(1, n_req)
    def _(k):
        pl.semaphore_signal(barrier, inc=1, device_id={"req": req_peer(k)}, device_id_type=MESH)

    @pl.loop(1, n_head)
    def _(k):
        pl.semaphore_signal(barrier, inc=1, device_id={"head": head_peer(k)}, device_id_type=MESH)

    @pl.loop(0, n_head)
    def _(k):
        pl.semaphore_signal(
            barrier, inc=1, device_id={"section": 1 - sec, "head": head_peer(k)}, device_id_type=MESH
        )

    pl.semaphore_wait(barrier, n_req - 1 + n_head - 1 + n_head)

    for j in range(2):
        owner = j * half

        @pl.when(me == owner)
        def _(j=j):
            csl[j] = cs_ref[0:8, :]

            @pl.loop(1, n_req)
            def _(k):
                peer = req_peer(k)
                req_copy(csl.at[j], csl.at[j], sc.at[j, k], rc.at[j], peer).start()

    @pl.when(sec == 0)
    def _():
        xin[...] = tok_ref[...]

    @pl.when(sec == 1)
    def _():
        @pl.loop(0, n_head)
        def _(k):
            pltpu.make_async_remote_copy(
                src_ref=xin.at[k], dst_ref=xin.at[k], send_sem=su.at[k], recv_sem=ru.at[k],
                device_id={"section": 0, "head": k}, device_id_type=MESH,
            ).wait_recv()

        pltpu.make_async_remote_copy(
            src_ref=xin, dst_ref=out_all, send_sem=sb.at[0], recv_sem=rb.at[0],
            device_id={"section": 0}, device_id_type=MESH,
        ).start()

    lanes128 = lax.broadcasted_iota(jnp.int32, (rows, HEAD), 1)

    x = xin[...].reshape(rows, cols).astype(F32)
    squares = jnp.sum(x * x, axis=1, keepdims=True)
    xg[...] = (x * gain1_ref[...].astype(F32)).astype(BF16)
    pair = split_two(squares, lanes128)
    send1[:, :, qw + 2 * HEAD :] = pair.reshape(n_req, 16, HEAD)
    loads[0].wait()

    @pl.loop(0, (qw + 2 * HEAD) // 256)
    def _(c):
        at = pl.ds(pl.multiple_of(c * 256, 256), 256)
        part = jnp.dot(xg[...], wqkv[:, at], preferred_element_type=F32)
        send1[:, :, at] = part.astype(BF16).reshape(n_req, 16, 256)

    spread(req_copy, n_req, req_peer, lambda p: send1.at[p], recv1, s1, r1, me)

    for j in range(2):
        row = send1[j * half].astype(F32)[0:1]
        for h in range(heads):
            ext32[j * 8 + h : j * 8 + h + 1, 0:HEAD] = row[:, h * HEAD : (h + 1) * HEAD]
        ext32[j * 8 : j * 8 + 8, HEAD:] = jnp.broadcast_to(row[:, qw + 2 * HEAD :], (8, HEAD))
    exts[me] = ext32[...].astype(BF16)
    spread(req_copy, n_req, req_peer, lambda p: exts.at[me], exts, se, re, me)
    recv1[me] = send1[me]

    r_id = lax.broadcasted_iota(jnp.int32, (16 * heads, 16), 0) & 15
    k_id = lax.broadcasted_iota(jnp.int32, (16 * heads, 16), 1)
    lens = jnp.broadcast_to(len_ref[...].astype(F32), (16 * heads, 16))
    seg_end = jnp.sum(jnp.where(k_id <= r_id, lens, 0.0), axis=1, keepdims=True).astype(jnp.int32)
    seg_start = jnp.sum(jnp.where(k_id < r_id, lens, 0.0), axis=1, keepdims=True).astype(jnp.int32)

    for j in range(2):

        @pl.when(me != j * half)
        def _(j=j):
            req_copy(csl.at[j], csl.at[j], sc.at[j, 1], rc.at[j], me).wait_recv()

    arrived(req_copy, n_req, req_peer, exts, se, re)
    total = exts[0].astype(F32)
    for p in range(1, n_req):
        total = total + exts[p].astype(F32)
    far_scale = lax.rsqrt((total[:, HEAD : HEAD + 1] + total[:, HEAD + 64 : HEAD + 65]) / width + EPSILON)
    table = jnp.concatenate(
        [jnp.broadcast_to(csl[0][0:1], (8, 2 * HEAD)), jnp.broadcast_to(csl[1][0:1], (8, 2 * HEAD))], axis=0
    )
    far_query = rope(total[:, :HEAD] * far_scale, table).astype(BF16)
    loads[1].wait()
    loads[2].wait()
    chunk = min(512, slots)
    n_chunk = slots // chunk
    contract = (((1,), (1,)), ((), ()))
    low_half = lax.broadcasted_iota(jnp.int32, (16, chunk), 0) < 8
    live = jnp.where(low_half, split_ref[0, 0], split_ref[1, 0])

    def far_first(c, best):
        at = pl.ds(pl.multiple_of(c * chunk, chunk), chunk)
        a = lax.dot_general(far_query, far[0, at, 0:HEAD], contract, preferred_element_type=F32)
        b = lax.dot_general(far_query, far[1, at, 0:HEAD], contract, preferred_element_type=F32)
        slot = lax.broadcasted_iota(jnp.int32, (16, chunk), 1) + c * chunk
        value = jnp.where(slot < live, jnp.where(low_half, a, b) * scale, NEG)
        fscore[:, at] = value
        return jnp.maximum(best, jnp.max(value, axis=1, keepdims=True))

    far_max = lax.fori_loop(0, n_chunk, far_first, jnp.full((16, 1), NEG, F32))
    low_rows = lax.broadcasted_iota(jnp.int32, (16, HEAD), 0) < 8

    def far_second(c, carry):
        totals, summed = carry
        at = pl.ds(pl.multiple_of(c * chunk, chunk), chunk)
        w = jnp.exp(fscore[:, at] - far_max).astype(BF16)
        a = jnp.dot(w, far[0, at, HEAD:], preferred_element_type=F32)
        b = jnp.dot(w, far[1, at, HEAD:], preferred_element_type=F32)
        totals = totals + jnp.sum(w.astype(F32), axis=1, keepdims=True)
        return totals, summed + jnp.where(low_rows, a, b)

    far_totals, far_sum = lax.fori_loop(
        0, n_chunk, far_second, (jnp.zeros((16, 1), F32), jnp.zeros((16, HEAD), F32))
    )
    far_out = far_sum / far_totals
    far_lse = jnp.broadcast_to(far_max + jnp.log(far_totals), (16, HEAD))

    arrived(req_copy, n_req, req_peer, recv1, s1, r1)

    def total_of(ref, at):
        value = ref[0, :, at].astype(F32)
        for p in range(1, ref.shape[0]):
            value = value + ref[p, :, at].astype(F32)
        return value

    stat = total_of(recv1, pl.ds(qw + 2 * HEAD, HEAD))
    row_scale = lax.rsqrt((stat[:, 0:1] + stat[:, 64:65]) / width + EPSILON)
    cs = cs_ref[...]

    @pl.loop(0, heads)
    def _(h):
        at = pl.ds(pl.multiple_of(h * HEAD, HEAD), HEAD)
        qbuf[h] = rope(total_of(recv1, at) * row_scale, cs).astype(BF16)

    new_key = rope(total_of(recv1, pl.ds(qw, HEAD)) * row_scale, cs).astype(BF16)
    new_value = (total_of(recv1, pl.ds(qw + HEAD, HEAD)) * row_scale).astype(BF16)
    queries = qbuf[...].reshape(heads * 16, HEAD)
    keys = jnp.concatenate([new_key.astype(F32)] * heads, axis=0)
    values = jnp.concatenate([new_value.astype(F32)] * heads, axis=0)
    own = jnp.sum(queries.astype(F32) * keys, axis=1, keepdims=True) * scale

    def near_first(c, best):
        at = pl.ds(pl.multiple_of(c * chunk, chunk), chunk)
        s = lax.dot_general(queries, pack[at, 0:HEAD], contract, preferred_element_type=F32)
        slot = lax.broadcasted_iota(jnp.int32, (heads * 16, chunk), 1) + c * chunk
        value = jnp.where((slot >= seg_start) & (slot < seg_end), s * scale, NEG)
        score[:, at] = value
        return jnp.maximum(best, jnp.max(value, axis=1, keepdims=True))

    row_max = lax.fori_loop(0, n_chunk, near_first, own)
    own_weight = jnp.exp(own - row_max).astype(BF16).astype(F32)

    def near_second(c, carry):
        totals, summed = carry
        at = pl.ds(pl.multiple_of(c * chunk, chunk), chunk)
        w = jnp.exp(score[:, at] - row_max).astype(BF16)
        summed = summed + jnp.dot(w, pack[at, HEAD:], preferred_element_type=F32)
        return totals + jnp.sum(w.astype(F32), axis=1, keepdims=True), summed

    totals, summed = lax.fori_loop(0, n_chunk, near_second, (own_weight, own_weight * values))
    attended = summed / totals
    att[...] = attended
    lse[...] = jnp.broadcast_to(row_max + jnp.log(totals), (heads * 16, HEAD))
    for h in range(heads):
        rows_all[me, :, h * HEAD : (h + 1) * HEAD] = attended[h * 16 : (h + 1) * 16].astype(BF16)
    spread(req_copy, n_req, req_peer, lambda p: rows_all.at[me], rows_all, s2, r2, me)

    first_out = att[pl.ds(0, heads, stride=16), :]
    first_lse = lse[pl.ds(0, heads, stride=16), :]
    near_out = jnp.concatenate([first_out, first_out], axis=0)
    near_lse = jnp.concatenate([first_lse, first_lse], axis=0)
    which = lax.broadcasted_iota(jnp.int32, (16, HEAD), 0)
    owned = jnp.where(which < 8, 0, half) == me
    peak = jnp.maximum(far_lse, near_lse)
    fa = jnp.exp(far_lse - peak)
    na = jnp.exp(near_lse - peak)
    both_out = (fa * far_out + na * near_out) / (fa + na)
    part_out = jnp.where(owned, both_out, far_out)
    part_lse = jnp.where(owned, peak + jnp.log(fa + na), far_lse)
    lane = lax.broadcasted_iota(jnp.int32, (16, HEAD), 1)
    high = part_lse.astype(BF16).astype(F32)
    middle = (part_lse - high).astype(BF16).astype(F32)
    low = part_lse - high - middle
    far_all[me, :, 0:HEAD] = part_out.astype(BF16)
    far_all[me, :, HEAD:] = jnp.where(lane < 32, high, jnp.where(lane < 64, middle, low)).astype(BF16)
    spread(req_copy, n_req, req_peer, lambda p: far_all.at[me], far_all, sl, rl, me)

    arrived(req_copy, n_req, req_peer, far_all, sl, rl)
    parts = []
    for p in range(n_req):
        part = far_all[p].astype(F32)
        parts.append(part[:, HEAD : HEAD + 1] + part[:, HEAD + 32 : HEAD + 33] + part[:, HEAD + 64 : HEAD + 65])
    peak = functools.reduce(jnp.maximum, parts)
    den = jnp.zeros((16, 1), F32)
    num = jnp.zeros((16, HEAD), F32)
    for p in range(n_req):
        w = jnp.exp(parts[p] - peak)
        den = den + w
        num = num + w * far_all[p, :, 0:HEAD].astype(F32)
    long_out = num / den
    arrived(req_copy, n_req, req_peer, rows_all, s2, r2)
    first = lax.broadcasted_iota(jnp.int32, (16, qw), 0) == 0
    for j in range(2):
        flat = jnp.concatenate([long_out[j * 8 + h : j * 8 + h + 1] for h in range(heads)], axis=1)
        block = rows_all[j * half].astype(F32)
        rows_mixed = jnp.where(first, jnp.broadcast_to(flat, (16, qw)), block).astype(BF16)
        xg_rows = rows_mixed
        if j == 0:
            mixed0 = xg_rows
        else:
            mixed1 = xg_rows

    loads[3].wait()
    send_rows = [mixed0 if g == 0 else mixed1 if g == half else rows_all[g] for g in range(n_req)]
    lhs = jnp.concatenate(send_rows, axis=0)

    n_tile = min(256, cols)

    for c in range(cols // n_tile):
        at = pl.ds(c * n_tile, n_tile)
        part = jnp.dot(lhs, wo[:, at], preferred_element_type=F32)
        send3[:, :, at] = part.astype(BF16).reshape(n_head, blk, n_tile)

    spread(head_copy, n_head, head_peer, lambda p: send3.at[p], recv3, s3, r3, mz)
    recv3[mz] = send3[mz]
    arrived(head_copy, n_head, head_peer, recv3, s3, r3)
    residual = xin[mz].astype(F32) + total_of(recv3, pl.ds(0, cols))
    res_all[mz] = residual.astype(BF16)
    spread(head_copy, n_head, head_peer, lambda p: res_all.at[mz], res_all, s4, r4, mz)
    arrived(head_copy, n_head, head_peer, res_all, s4, r4)

    x = res_all[...].reshape(rows, cols).astype(F32)
    squares = jnp.sum(x * x, axis=1, keepdims=True)
    xg[...] = (x * gain2_ref[...].astype(F32)).astype(BF16)
    pair = split_two(squares, lanes128)
    send5[:, :, 2 * ff :] = pair.reshape(n_req, 16, HEAD)
    loads[4].wait()

    @pl.loop(0, 2 * ff // 256)
    def _(c):
        at = pl.ds(pl.multiple_of(c * 256, 256), 256)
        part = jnp.dot(xg[...], wgu[:, at], preferred_element_type=F32)
        send5[:, :, at] = part.astype(BF16).reshape(n_req, 16, 256)

    spread(req_copy, n_req, req_peer, lambda p: send5.at[p], recv5, s5, r5, me)
    recv5[me] = send5[me]
    arrived(req_copy, n_req, req_peer, recv5, s5, r5)
    stat = total_of(recv5, pl.ds(2 * ff, HEAD))
    row_scale = lax.rsqrt((stat[:, 0:1] + stat[:, 64:65]) / width + EPSILON)

    @pl.loop(0, ff // 256)
    def _(c):
        at = pl.ds(pl.multiple_of(c * 256, 256), 256)
        up_at = pl.ds(pl.multiple_of(ff + c * 256, 256), 256)
        gate = total_of(recv5, at) * row_scale
        up = total_of(recv5, up_at) * row_scale
        hid_all[me, :, at] = (gate / (1.0 + jnp.exp(-gate)) * up).astype(BF16)

    spread(req_copy, n_req, req_peer, lambda p: hid_all.at[me], hid_all, s6, r6, me)
    arrived(req_copy, n_req, req_peer, hid_all, s6, r6)

    loads[5].wait()

    @pl.loop(0, cols // n_tile)
    def _(c):
        at = pl.ds(pl.multiple_of(c * n_tile, n_tile), n_tile)
        part = jnp.dot(hid_all[...].reshape(rows, ff), wd[:, at], preferred_element_type=F32)
        send7[:, :, at] = part.astype(BF16).reshape(n_head, blk, n_tile)

    spread(head_copy, n_head, head_peer, lambda p: send7.at[p], recv7, s7, r7, mz)
    recv7[mz] = send7[mz]
    arrived(head_copy, n_head, head_peer, recv7, s7, r7)
    oblk[...] = (res_all[mz].astype(F32) + total_of(recv7, pl.ds(0, cols))).astype(BF16)

    def hand_over(k):
        peer = head_peer(k)
        return pltpu.make_async_remote_copy(
            src_ref=oblk, dst_ref=xin.at[mz], send_sem=su.at[k], recv_sem=ru.at[mz],
            device_id={"section": 1, "head": peer}, device_id_type=MESH,
        )

    @pl.when(sec == 0)
    def _():
        @pl.loop(0, n_head)
        def _(k):
            hand_over(k).start()

        pltpu.make_async_remote_copy(
            src_ref=xin, dst_ref=out_all, send_sem=sb.at[0], recv_sem=rb.at[0],
            device_id={"section": 1}, device_id_type=MESH,
        ).wait_recv()

        @pl.loop(0, n_head)
        def _(k):
            hand_over(k).wait_send()

    @pl.when(sec == 1)
    def _():
        out_all[mz] = oblk[...]
        spread(head_copy, n_head, head_peer, lambda p: oblk, out_all, s8, r8, mz)
        arrived(head_copy, n_head, head_peer, out_all, s8, r8)
        sent(head_copy, n_head, head_peer, lambda p: oblk, out_all, s8, r8, mz)
        pltpu.make_async_remote_copy(
            src_ref=xin, dst_ref=out_all, send_sem=sb.at[0], recv_sem=rb.at[0],
            device_id={"section": 0}, device_id_type=MESH,
        ).wait_send()

    out_ref[...] = out_all[...]

    for j in range(2):

        @pl.when(me == j * half)
        def _(j=j):
            @pl.loop(1, n_req)
            def _(k):
                peer = req_peer(k)
                req_copy(csl.at[j], csl.at[j], sc.at[j, k], rc.at[j], peer).wait_send()

    sent(req_copy, n_req, req_peer, lambda p: send1.at[p], recv1, s1, r1, me)
    sent(req_copy, n_req, req_peer, lambda p: exts.at[me], exts, se, re, me)
    sent(req_copy, n_req, req_peer, lambda p: rows_all.at[me], rows_all, s2, r2, me)
    sent(req_copy, n_req, req_peer, lambda p: far_all.at[me], far_all, sl, rl, me)
    sent(head_copy, n_head, head_peer, lambda p: send3.at[p], recv3, s3, r3, mz)
    sent(head_copy, n_head, head_peer, lambda p: res_all.at[mz], res_all, s4, r4, mz)
    sent(req_copy, n_req, req_peer, lambda p: send5.at[p], recv5, s5, r5, me)
    sent(req_copy, n_req, req_peer, lambda p: hid_all.at[me], hid_all, s6, r6, me)
    sent(head_copy, n_head, head_peer, lambda p: send7.at[p], recv7, s7, r7, mz)


def rope_table(position):
    half = HEAD // 2
    freq_ids = jnp.arange(half).astype(F32)
    inverse = 1.0 / 10000.0 ** (freq_ids * 2.0 / HEAD)
    angles = position.astype(F32)[:, None] * inverse[None, :]
    cosine, sine = jnp.cos(angles), jnp.sin(angles)
    return jnp.concatenate([cosine, cosine, -sine, sine], axis=-1)


def local(
    tokens,
    attention_gain,
    query_key_value_weight,
    head_output_weight,
    feedforward_gain,
    gate_up,
    down_weight,
    packed_cache,
    long_cache,
    lengths,
    long_split,
):
    n_req = lax.axis_size("req")
    n_head = lax.axis_size("head")
    group = lax.axis_index("req")
    rows, cols = tokens.shape
    blk = rows // n_head
    qkv = query_key_value_weight.shape[3]
    qw = head_output_weight.shape[2]
    ff = down_weight.shape[1]
    slots = packed_cache.shape[1]
    far_slots = long_cache.shape[2]
    assert slots == far_slots and rows == n_req * 16
    is_long = (jnp.arange(16) == 0) & ((group == 0) | (group == n_req // 2))
    table = rope_table(lengths[0] + jnp.where(is_long, LONG, 0).astype(jnp.int32))
    vmem = pl.BlockSpec(memory_space=pltpu.VMEM)
    hbm = pl.BlockSpec(memory_space=pl.ANY)
    smem = pl.BlockSpec(memory_space=pltpu.SMEM)

    def dma(*shape):
        return pltpu.SemaphoreType.DMA(shape)

    out = pl.pallas_call(
        functools.partial(kernel, (n_req, n_head, cols * n_req)),
        out_shape=jax.ShapeDtypeStruct((n_head, blk, cols), BF16),
        in_specs=[smem, vmem, vmem, hbm, hbm, vmem, hbm, hbm, hbm, hbm, vmem, vmem],
        out_specs=vmem,
        scratch_shapes=[
            pltpu.VMEM((cols, qkv), BF16),
            pltpu.VMEM((qw, cols), BF16),
            pltpu.VMEM((cols, 2 * ff), BF16),
            pltpu.VMEM((ff, cols), BF16),
            pltpu.VMEM((slots, 2 * HEAD), BF16),
            pltpu.VMEM((2, far_slots, 2 * HEAD), BF16),
            pltpu.VMEM((n_head, blk, cols), BF16),
            pltpu.VMEM((rows, cols), BF16),
            pltpu.VMEM((n_req, 16, qkv + HEAD), BF16),
            pltpu.VMEM((n_req, 16, qkv + HEAD), BF16),
            pltpu.VMEM((16, 2 * HEAD), F32),
            pltpu.VMEM((n_req, 16, 2 * HEAD), BF16),
            pltpu.VMEM((2, 8, 2 * HEAD), F32),
            pltpu.VMEM((8, 16, HEAD), BF16),
            pltpu.VMEM((128, slots), F32),
            pltpu.VMEM((128, HEAD), F32),
            pltpu.VMEM((128, HEAD), F32),
            pltpu.VMEM((16, far_slots), F32),
            pltpu.VMEM((n_req, 16, qw), BF16),
            pltpu.VMEM((n_req, 16, 2 * HEAD), BF16),
            pltpu.VMEM((n_head, blk, cols), BF16),
            pltpu.VMEM((n_head, blk, cols), BF16),
            pltpu.VMEM((n_head, blk, cols), BF16),
            pltpu.VMEM((n_req, 16, 2 * ff + HEAD), BF16),
            pltpu.VMEM((n_req, 16, 2 * ff + HEAD), BF16),
            pltpu.VMEM((n_req, 16, ff), BF16),
            pltpu.VMEM((n_head, blk, cols), BF16),
            pltpu.VMEM((n_head, blk, cols), BF16),
            pltpu.VMEM((blk, cols), BF16),
            pltpu.VMEM((n_head, blk, cols), BF16),
            dma(6),
            dma(n_req), dma(n_req),
            dma(n_req), dma(n_req),
            dma(2, n_req), dma(2),
            dma(n_req), dma(n_req),
            dma(n_req), dma(n_req),
            dma(n_head), dma(n_head),
            dma(n_head), dma(n_head),
            dma(n_req), dma(n_req),
            dma(n_req), dma(n_req),
            dma(n_head), dma(n_head),
            dma(n_head), dma(n_head),
            dma(n_head), dma(n_head),
            dma(1), dma(1),
        ],
        compiler_params=pltpu.CompilerParams(
            collective_id=0, has_side_effects=True, vmem_limit_bytes=56 * 2**20
        ),
    )(
        long_split,
        tokens.reshape(n_head, blk, cols),
        attention_gain,
        query_key_value_weight.reshape(cols, qkv),
        head_output_weight.reshape(qw, cols),
        feedforward_gain,
        gate_up.reshape(cols, 2 * ff),
        down_weight.reshape(ff, cols),
        packed_cache.reshape(slots, 2 * HEAD),
        long_cache.reshape(2, far_slots, 2 * HEAD),
        lengths,
        table,
    )
    return out.reshape(1, rows, cols)


def solution(mesh):
    placed = (
        P(None, "req"),
        P("section", "req"),
        P("section", "req", "head", None),
        P("section", "head", None, "req"),
        P("section", "req"),
        P("section", "req", None, "head"),
        P("section", "head", "req"),
        P("section", "req", "head", None),
        P("section", None, "req", "head", None),
        P("req", None),
        P(None, "req"),
    )
    return jax.shard_map(
        local, mesh=mesh, in_specs=placed, out_specs=P("section", None, "req"), check_vma=False
    )
```

```python
import functools
import math

import jax
import jax.numpy as jnp
import numpy as np
from jax import lax
from jax.experimental import pallas as pl
from jax.experimental.pallas import tpu as pltpu
from jax.sharding import PartitionSpec as P

HEAD = 128
HEADS = 8
LONG = 16384
EPSILON = 1e-05
NEG = -1e30
F32 = jnp.float32
BF16 = jnp.bfloat16
MESH = pl.DeviceIdType.MESH
SIDE = 4


def split_two(value, lanes):
    high = value.astype(BF16).astype(F32)
    return jnp.where(lanes < 64, high, value - high).astype(BF16)


def rope(block, table):
    swapped = jnp.concatenate([block[:, HEAD // 2 :], block[:, : HEAD // 2]], axis=1)
    return block * table[0] + swapped * table[1]


def rope_tables(position, inverse):
    angles = position * inverse
    lane = lax.broadcasted_iota(jnp.int32, angles.shape, 1)
    sine = jnp.sin(angles)
    return jnp.cos(angles), jnp.where(lane < HEAD // 2, -sine, sine)


def kernel(dims, ff_parts, split_ref, tok_hbm, gain1_ref, wqkv_hbm, wo_hbm, gain2_ref, raw_hbm, wd_hbm, pack_hbm, far_hbm,
           len_ref, inv_ref, out_ref, scratch):
    n_req, n_head, width = dims
    s = scratch
    sec = lax.axis_index("section")
    me = lax.axis_index("req")
    mz = lax.axis_index("head")
    mx, my = lax.div(me, SIDE), lax.rem(me, SIDE)
    xin = s["xin"]
    n_half, _, blk, hcols = xin.shape
    cols = n_half * hcols
    rows = n_head * blk
    slots = s["pack"].shape[0]
    qw = HEADS * HEAD
    ff = s["wd"].shape[0]
    scale = 1.0 / math.sqrt(HEAD)
    mid = n_req // 2
    stat_at = qw + 2 * HEAD
    ext_at = stat_at + HEAD

    def remote(source, target, name, where, peer):
        return pltpu.make_async_remote_copy(
            src_ref=source, dst_ref=target, send_sem=s["ss_" + name].at[where], recv_sem=s["rs_" + name].at[where],
            device_id=peer, device_id_type=MESH,
        )

    def req_peer(k):
        return {"req": lax.rem(mx + lax.div(k, SIDE), SIDE) * SIDE + lax.rem(my + lax.rem(k, SIDE), SIDE)}

    def head_peer(k):
        return {"head": lax.rem(mz + k, n_head)}

    def spread_req(name, source, target, where=0):
        @pl.loop(1, n_req)
        def _(k):
            peer = req_peer(k)
            remote(source(peer["req"]), target.at[me], name, where, peer).start()

    def spread_head(name, source, target, where=0):
        @pl.loop(1, n_head)
        def _(k):
            peer = head_peer(k)
            remote(source(peer["head"]), target.at[mz], name, where, peer).start()

    def arrived(name, target, count, where=0):
        whole = target.at[pl.ds(0, count)]
        remote(whole, whole, name, where, {"section": 1 - sec}).wait_recv()

    def sent(name, source, count, where=0):
        whole = source.at[pl.ds(0, count)]
        remote(whole, whole, name, where, {"section": 1 - sec}).wait_send()

    def load(source, target, n):
        return pltpu.make_async_copy(source, target, s["wsem"].at[n])

    load_qkv = load(wqkv_hbm, s["wqkv"], 0)
    load_raw = load(raw_hbm, s["raw"], 1)
    load_pack = load(pack_hbm, s["pack"], 2)
    load_far = load(far_hbm, s["far"], 3)
    load_wo = load(wo_hbm, s["wo"], 4)
    load_wd = load(wd_hbm, s["wd"], 5)
    load_qkv.start()

    @pl.when(sec == 0)
    def _():
        for h in range(n_half):
            load(tok_hbm.at[:, :, pl.ds(h * hcols, hcols)], xin.at[h], 6 + h).start()

    barrier = pltpu.get_barrier_semaphore()

    @pl.loop(1, n_req)
    def _(k):
        pl.semaphore_signal(barrier, inc=1, device_id=req_peer(k), device_id_type=MESH)

    @pl.loop(1, n_head)
    def _(k):
        pl.semaphore_signal(barrier, inc=1, device_id=head_peer(k), device_id_type=MESH)

    @pl.loop(0, n_head)
    def _(k):
        pl.semaphore_signal(barrier, inc=1, device_id={"section": 1 - sec, **head_peer(k)}, device_id_type=MESH)

    for other in (load_raw, load_pack, load_far, load_wo, load_wd):
        other.start()

    def lane_sum(mask, shape):
        lens = jnp.broadcast_to(len_ref[...].astype(F32), shape)
        return jnp.sum(jnp.where(mask, lens, 0.0), axis=1, keepdims=True)

    r16 = lax.broadcasted_iota(jnp.int32, (16, 16), 0)
    k16 = lax.broadcasted_iota(jnp.int32, (16, 16), 1)
    is_long = (lax.broadcasted_iota(jnp.int32, (16, 1), 0) == 0) & ((me == 0) | (me == mid))
    position = lane_sum(k16 == r16, (16, 16)) + jnp.where(is_long, float(LONG), 0.0)

    lanes = lax.broadcasted_iota(jnp.int32, (rows, HEAD), 1)
    lane16 = lax.broadcasted_iota(jnp.int32, (16, HEAD), 1)

    def normed(source, gain_ref):
        squares = jnp.zeros((rows, 1), F32)
        for h in range(n_half):
            at = pl.ds(h * hcols, hcols)
            x = source[h].reshape(rows, hcols).astype(F32)
            squares = squares + jnp.sum(x * x, axis=1, keepdims=True)
            s["xg"][:, at] = (x * gain_ref[:, at].astype(F32)).astype(BF16)
        return squares

    def first_products():
        squares = normed(xin, gain1_ref)
        s["send1"][:, :, stat_at : stat_at + HEAD] = split_two(squares, lanes).reshape(n_req, 16, HEAD)
        load_qkv.wait()

        @pl.loop(0, stat_at // 256)
        def _(c):
            at = pl.ds(pl.multiple_of(c * 256, 256), 256)
            part = jnp.dot(s["xg"][...], s["wqkv"][:, at], preferred_element_type=F32)
            s["send1"][:, :, at] = part.astype(BF16).reshape(n_req, 16, 256)

        ext = s["ext"]
        for j in range(2):
            row = s["send1"][j * mid].astype(F32)[0:1]
            for h in range(HEADS):
                ext[j * 8 + h : j * 8 + h + 1, 0:HEAD] = row[:, h * HEAD : (h + 1) * HEAD]
            ext[j * 8 : j * 8 + 8, HEAD:] = jnp.broadcast_to(row[:, stat_at : stat_at + HEAD], (8, HEAD))
        first = position[0:1]
        upper = jnp.floor(first * (1.0 / 256.0))
        lower = first - 256.0 * upper
        tail = ext[:, HEAD:]
        stats = jnp.where(lane16 < 32, tail[:, 0:1], tail[:, 64:65])
        places = jnp.where(lane16 < 96, upper, lower)
        tail = jnp.where(lane16 < 64, stats, places).astype(BF16)
        head = ext[:, 0:HEAD].astype(BF16)
        for g in range(n_req):
            s["send1"][g, :, ext_at : ext_at + HEAD] = head
            s["send1"][g, :, ext_at + HEAD :] = tail

    def split_gate():
        load_raw.wait()
        raw, wgu = s["raw"], s["wgu"]

        @pl.loop(0, cols // 16)
        def _(k):
            at = pl.ds(pl.multiple_of(k * 16, 16), 16)
            for c in range(ff // HEAD):
                source = pl.ds(c * HEAD, HEAD)
                wgu[at, pl.ds(c * 256, HEAD)] = raw[at, 0, source]
                wgu[at, pl.ds(c * 256 + HEAD, HEAD)] = raw[at, 1, source]

    @pl.when(sec == 0)
    def _():
        for h in range(n_half):
            load(tok_hbm.at[:, :, pl.ds(h * hcols, hcols)], xin.at[h], 6 + h).wait()
        first_products()

    pl.semaphore_wait(barrier, n_req - 1 + n_head - 1 + n_head)

    @pl.when(sec == 1)
    def _():
        split_gate()
        for h in range(n_half):
            remote(xin.at[h], xin.at[h], "in", h, {"section": 0}).wait_recv()
        remote(xin, s["out"], "back", 0, {"section": 0}).start()
        first_products()

    spread_req("p1", lambda p: s["send1"].at[p], s["recv1"])
    s["recv1"][me] = s["send1"][me]

    @pl.when(sec == 0)
    def _():
        split_gate()

    own_table = rope_tables(position, inv_ref[...])
    r_id = lax.broadcasted_iota(jnp.int32, (16 * HEADS, 16), 0) & 15
    k_id = lax.broadcasted_iota(jnp.int32, (16 * HEADS, 16), 1)
    seg_end = lane_sum(k_id <= r_id, (16 * HEADS, 16)).astype(jnp.int32)
    seg_start = lane_sum(k_id < r_id, (16 * HEADS, 16)).astype(jnp.int32)
    load_pack.wait()
    load_far.wait()
    pack, far = s["pack"], s["far"]
    recv1 = s["recv1"]
    arrived("p1", recv1, n_req - 1)

    def total_of(ref, at):
        value = ref[0, :, at].astype(F32)
        for p in range(1, ref.shape[0]):
            value = value + ref[p, :, at].astype(F32)
        return value

    stat = total_of(recv1, pl.ds(stat_at, HEAD))
    row_scale = lax.rsqrt((stat[:, 0:1] + stat[:, 64:65]) / width + EPSILON)

    @pl.loop(0, HEADS)
    def _(h):
        at = pl.ds(pl.multiple_of(h * HEAD, HEAD), HEAD)
        s["q"][h] = rope(total_of(recv1, at) * row_scale, own_table).astype(BF16)

    new_key = rope(total_of(recv1, pl.ds(qw, HEAD)) * row_scale, own_table).astype(BF16)
    new_value = (total_of(recv1, pl.ds(qw + HEAD, HEAD)) * row_scale).astype(BF16)
    queries = s["q"][...].reshape(HEADS * 16, HEAD)
    keys = jnp.concatenate([new_key.astype(F32)] * HEADS, axis=0)
    values = jnp.concatenate([new_value.astype(F32)] * HEADS, axis=0)
    own = jnp.sum(queries.astype(F32) * keys, axis=1, keepdims=True) * scale

    total = total_of(recv1, pl.ds(ext_at, HEAD))
    tail = total_of(recv1, pl.ds(ext_at + HEAD, HEAD))
    far_scale = lax.rsqrt((tail[:, 0:1] + tail[:, 32:33]) / width + EPSILON)
    low8 = lax.broadcasted_iota(jnp.int32, (16, HEAD), 0) < 8
    places = jnp.where(
        low8, recv1[0, :, ext_at + HEAD :].astype(F32), recv1[mid, :, ext_at + HEAD :].astype(F32)
    )
    far_table = rope_tables(places[:, 64:65] * 256.0 + places[:, 96:97], inv_ref[...])
    far_query = rope(total * far_scale, far_table).astype(BF16)

    chunk = min(512, slots)
    n_chunk = slots // chunk
    contract = (((1,), (1,)), ((), ()))
    low_chunk = lax.broadcasted_iota(jnp.int32, (16, chunk), 0) < 8
    live = jnp.where(low_chunk, split_ref[0, 0], split_ref[0, 1])

    def scores_of(c, best):
        far_best, near_best = best
        at = pl.ds(pl.multiple_of(c * chunk, chunk), chunk)
        a = lax.dot_general(far_query, far[0, at, 0:HEAD], contract, preferred_element_type=F32)
        b = lax.dot_general(far_query, far[1, at, 0:HEAD], contract, preferred_element_type=F32)
        slot = lax.broadcasted_iota(jnp.int32, (16, chunk), 1) + c * chunk
        value = jnp.where(slot < live, jnp.where(low_chunk, a, b) * scale, NEG)
        s["fscore"][:, at] = value
        far_best = jnp.maximum(far_best, jnp.max(value, axis=1, keepdims=True))
        near = lax.dot_general(queries, pack[at, 0:HEAD], contract, preferred_element_type=F32)
        slot = lax.broadcasted_iota(jnp.int32, (HEADS * 16, chunk), 1) + c * chunk
        value = jnp.where((slot >= seg_start) & (slot < seg_end), near * scale, NEG)
        s["score"][:, at] = value
        return far_best, jnp.maximum(near_best, jnp.max(value, axis=1, keepdims=True))

    far_max, row_max = lax.fori_loop(0, n_chunk, scores_of, (jnp.full((16, 1), NEG, F32), own))
    own_weight = jnp.exp(own - row_max).astype(BF16).astype(F32)

    def sums_of(c, carry):
        far_totals, far_sum, totals, summed = carry
        at = pl.ds(pl.multiple_of(c * chunk, chunk), chunk)
        w = jnp.exp(s["fscore"][:, at] - far_max).astype(BF16)
        a = jnp.dot(w, far[0, at, HEAD:], preferred_element_type=F32)
        b = jnp.dot(w, far[1, at, HEAD:], preferred_element_type=F32)
        far_totals = far_totals + jnp.sum(w.astype(F32), axis=1, keepdims=True)
        far_sum = far_sum + jnp.where(low8, a, b)
        w = jnp.exp(s["score"][:, at] - row_max).astype(BF16)
        summed = summed + jnp.dot(w, pack[at, HEAD:], preferred_element_type=F32)
        return far_totals, far_sum, totals + jnp.sum(w.astype(F32), axis=1, keepdims=True), summed

    far_totals, far_sum, totals, summed = lax.fori_loop(
        0, n_chunk, sums_of,
        (jnp.zeros((16, 1), F32), jnp.zeros((16, HEAD), F32), own_weight, own_weight * values),
    )
    far_out = far_sum / far_totals
    far_lse = jnp.broadcast_to(far_max + jnp.log(far_totals), (16, HEAD))
    attended = summed / totals
    s["att"][...] = attended
    s["lse"][...] = jnp.broadcast_to(row_max + jnp.log(totals), (HEADS * 16, HEAD))
    mixed = s["mixed"]
    for h in range(HEADS):
        mixed[me, :, h * HEAD : (h + 1) * HEAD] = attended[h * 16 : (h + 1) * 16].astype(BF16)

    first_out = s["att"][pl.ds(0, HEADS, stride=16), :]
    first_lse = s["lse"][pl.ds(0, HEADS, stride=16), :]
    near_out = jnp.concatenate([first_out, first_out], axis=0)
    near_lse = jnp.concatenate([first_lse, first_lse], axis=0)
    owned = jnp.where(low8, 0, mid) == me
    peak = jnp.maximum(far_lse, near_lse)
    fa = jnp.exp(far_lse - peak)
    na = jnp.exp(near_lse - peak)
    part_out = jnp.where(owned, (fa * far_out + na * near_out) / (fa + na), far_out)
    part_lse = jnp.where(owned, peak + jnp.log(fa + na), far_lse)
    high = part_lse.astype(BF16).astype(F32)
    middle = (part_lse - high).astype(BF16).astype(F32)
    low = part_lse - high - middle
    mixed[me, :, qw : qw + HEAD] = part_out.astype(BF16)
    mixed[me, :, qw + HEAD :] = jnp.where(lane16 < 32, high, jnp.where(lane16 < 64, middle, low)).astype(BF16)
    spread_req("p2", lambda p: mixed.at[me], mixed)
    sent("p1", s["send1"], n_req - 1)
    load_wo.wait()
    arrived("p2", mixed, n_req - 1)

    parts = []
    for p in range(n_req):
        part = mixed[p, :, qw + HEAD :].astype(F32)
        parts.append(part[:, 0:1] + part[:, 32:33] + part[:, 64:65])
    peak = functools.reduce(jnp.maximum, parts)
    den = jnp.zeros((16, 1), F32)
    num = jnp.zeros((16, HEAD), F32)
    for p in range(n_req):
        w = jnp.exp(parts[p] - peak)
        den = den + w
        num = num + w * mixed[p, :, qw : qw + HEAD].astype(F32)
    long_out = num / den
    lhs = s["lhs"]
    lhs[...] = mixed[:, :, 0:qw]
    first = lax.broadcasted_iota(jnp.int32, (16, qw), 0) == 0
    for j in range(2):
        flat = jnp.concatenate([long_out[j * 8 + h : j * 8 + h + 1] for h in range(HEADS)], axis=1)
        block = mixed[j * mid, :, 0:qw].astype(F32)
        lhs[j * mid] = jnp.where(first, jnp.broadcast_to(flat, (16, qw)), block).astype(BF16)

    send3, recv3, res = s["send3"], s["recv3"], s["res"]
    for h in range(n_half):
        part = jnp.dot(lhs[...].reshape(rows, qw), s["wo"][:, pl.ds(h * hcols, hcols)], preferred_element_type=F32)
        send3[h] = part.astype(BF16).reshape(n_head, blk, hcols)
        spread_head("p3", lambda p, h=h: send3.at[h, p], recv3.at[h], h)
    sent("p2", mixed, n_req - 1)

    def block_total(buffer, mine, h):
        value = mine[h, mz].astype(F32)
        for k in range(1, n_head):
            value = value + buffer[h, lax.rem(mz + k, n_head)].astype(F32)
        return value

    for h in range(n_half):
        arrived("p3", recv3.at[h], n_head - 1, h)
        res[h, mz] = (xin[h, mz].astype(F32) + block_total(recv3, send3, h)).astype(BF16)
        spread_head("p4", lambda p, h=h: res.at[h, mz], res.at[h], h)
    for h in range(n_half):
        sent("p3", send3.at[h], n_head - 1, h)
    for h in range(n_half):
        arrived("p4", res.at[h], n_head - 1, h)

    squares = normed(res, gain2_ref)
    n_part = len(ff_parts)

    def along(side, k):
        if side == 0:
            c = lax.rem(mx + k, SIDE)
            return c, {"req": c * SIDE + my}
        c = lax.rem(my + k, SIDE)
        return c, {"req": mx * SIDE + c}

    coordinate = (mx, my)
    for g, (begin, end) in enumerate(ff_parts):
        buf = s[f"fs{g}"]

        @pl.loop(begin, end)
        def _(c, g=g, buf=buf, begin=begin):
            part = jnp.dot(
                s["xg"][...], s["wgu"][:, pl.ds(pl.multiple_of(c * 256, 256), 256)], preferred_element_type=F32
            ).astype(BF16).reshape(SIDE, SIDE, 16, 256)
            at = pl.ds(pl.multiple_of((c - begin) * 256, 256), 256)
            for a in range(SIDE):
                if g % 2 == 0:
                    buf[a, :, :, at] = part[a]
                else:
                    buf[a, :, :, at] = part[:, a]

        if g == 0:
            at = pl.ds((end - begin) * 256, HEAD)
            buf[:, :, :, at] = split_two(squares, lanes).reshape(SIDE, SIDE, 16, HEAD)
        for k in range(1, SIDE):
            c, peer = along(g % 2, k)
            remote(buf.at[c], s[f"fr{g}"].at[coordinate[g % 2]], "f1", g, peer).start()
    for h in range(n_half):
        sent("p4", res.at[h], n_head - 1, h)

    for g, (begin, end) in enumerate(ff_parts):
        side = g % 2
        buf, got, turn = s[f"fs{g}"], s[f"fr{g}"], s[f"ft{g}"]
        arrived("f1", got, SIDE - 1, g)
        mine = coordinate[side]

        @pl.loop(0, SIDE)
        def _(b, g=g, buf=buf, got=got, turn=turn, mine=mine, begin=begin, end=end):
            value = buf[mine, b].astype(F32)
            for k in range(1, SIDE):
                value = value + got[lax.rem(mine + k, SIDE), b].astype(F32)
            turn[b] = value.astype(BF16)
            if g == 0:
                stat = value[:, (end - begin) * 256 :]
                turn[b, :, pl.ds((end - begin) * 256, HEAD)] = split_two(stat[:, 0:1] + stat[:, 64:65], lane16)

        for k in range(1, SIDE):
            c, peer = along(1 - side, k)
            remote(turn.at[c], s[f"fu{g}"].at[coordinate[1 - side]], "f2", g, peer).start()

    ff_scale = None
    hid = (s["hid0"], s["hid1"])
    for g, (begin, end) in enumerate(ff_parts):
        side = g % 2
        turn, got = s[f"ft{g}"], s[f"fu{g}"]
        arrived("f2", got, SIDE - 1, g)
        mine = coordinate[1 - side]

        def turned(at, turn=turn, got=got, mine=mine):
            value = turn[mine, :, at].astype(F32)
            for k in range(1, SIDE):
                value = value + got[lax.rem(mine + k, SIDE), :, at].astype(F32)
            return value

        if g == 0:
            stat = turned(pl.ds((end - begin) * 256, HEAD))
            ff_scale = lax.rsqrt((stat[:, 0:1] + stat[:, 64:65]) / width + EPSILON)
        which = g // 2
        base = ff_parts[2 * which][0]
        for c in range(begin, end):
            both = turned(pl.ds((c - begin) * 256, 256)) * ff_scale
            gate, up = both[:, :HEAD], both[:, HEAD:]
            hid[which][me, :, pl.ds((c - base) * HEAD, HEAD)] = (gate / (1.0 + jnp.exp(-gate)) * up).astype(BF16)
        if g % 2 == 1:
            spread_req("p6", lambda p, which=which: hid[which].at[me], hid[which], which)
    for g in range(n_part):
        sent("f1", s[f"fs{g}"], SIDE - 1, g)
        sent("f2", s[f"ft{g}"], SIDE - 1, g)

    load_wd.wait()
    send7, recv7, oblk, out, down = s["send7"], s["recv7"], s["oblk"], s["out"], s["down"]
    wide0 = hid[0].shape[2]
    arrived("p6", hid[0], n_req - 1, 0)
    for h in range(n_half):
        at = pl.ds(h * hcols, hcols)
        down[:, at] = jnp.dot(hid[0][...].reshape(rows, wide0), s["wd"][pl.ds(0, wide0), at], preferred_element_type=F32)
    arrived("p6", hid[1], n_req - 1, 1)
    for h in range(n_half):
        at = pl.ds(h * hcols, hcols)
        part = down[:, at] + jnp.dot(
            hid[1][...].reshape(rows, ff - wide0), s["wd"][pl.ds(wide0, ff - wide0), at], preferred_element_type=F32
        )
        send7[h] = part.astype(BF16).reshape(n_head, blk, hcols)
        spread_head("p7", lambda p, h=h: send7.at[h, p], recv7.at[h], h)
    for which in range(2):
        sent("p6", hid[which], n_req - 1, which)

    def hand_over(k, h):
        return remote(oblk.at[h], xin.at[h, mz], "in", h, {"section": 1, **head_peer(k)})

    for h in range(n_half):
        arrived("p7", recv7.at[h], n_head - 1, h)
        oblk[h] = (res[h, mz].astype(F32) + block_total(recv7, send7, h)).astype(BF16)

        @pl.when(sec == 0)
        def _(h=h):
            @pl.loop(0, n_head)
            def _(k):
                hand_over(k, h).start()

        @pl.when(sec == 1)
        def _(h=h):
            out[h, mz] = oblk[h]
            spread_head("p8", lambda p: oblk.at[h], out.at[h], h)

    for h in range(n_half):
        sent("p7", send7.at[h], n_head - 1, h)

    @pl.when(sec == 0)
    def _():
        remote(xin, out, "back", 0, {"section": 1}).wait_recv()
        for h in range(n_half):
            remote(xin.at[h], xin.at[h], "in", h, {"section": 1}).wait_send()

    @pl.when(sec == 1)
    def _():
        for h in range(n_half):
            arrived("p8", out.at[h], n_head - 1, h)

    for h in range(n_half):
        out_ref[:, :, pl.ds(h * hcols, hcols)] = out[h]

    @pl.when(sec == 1)
    def _():
        for h in range(n_half):
            sent("p8", out.at[h], n_head - 1, h)
        remote(xin, out, "back", 0, {"section": 0}).wait_send()


def local(
    tokens,
    attention_gain,
    query_key_value_weight,
    head_output_weight,
    feedforward_gain,
    gate_up,
    down_weight,
    packed_cache,
    long_cache,
    lengths,
    long_split,
):
    n_req = lax.axis_size("req")
    n_head = lax.axis_size("head")
    rows, cols = tokens.shape
    blk = rows // n_head
    qkv = query_key_value_weight.shape[3]
    qw = head_output_weight.shape[2]
    ff = down_weight.shape[1]
    slots = packed_cache.shape[1]
    assert slots == long_cache.shape[2] and rows == n_req * 16 and n_req == SIDE * SIDE
    half = (2, n_head, blk, cols // 2)
    n = ff // HEAD
    cuts = (0, (2 * n + 6) // 7, (4 * n + 6) // 7, (11 * n + 12) // 14, n)
    ff_parts = tuple(zip(cuts[:-1], cuts[1:]))
    freq_ids = np.arange(HEAD // 2, dtype=np.float32)
    inverse = np.float32(1.0) / np.power(np.float32(10000.0), freq_ids * np.float32(2.0) / np.float32(HEAD))
    inverse = jnp.asarray(np.concatenate([inverse, inverse])[None].astype(np.float32))
    vmem = pl.BlockSpec(memory_space=pltpu.VMEM)
    hbm = pl.BlockSpec(memory_space=pl.ANY)
    smem = pl.BlockSpec(memory_space=pltpu.SMEM)
    scratch = dict(
        wqkv=pltpu.VMEM((cols, qkv), BF16),
        wo=pltpu.VMEM((qw, cols), BF16),
        raw=pltpu.VMEM((cols, 2, ff), BF16),
        wgu=pltpu.VMEM((cols, 2 * ff), BF16),
        wd=pltpu.VMEM((ff, cols), BF16),
        pack=pltpu.VMEM((slots, 2 * HEAD), BF16),
        far=pltpu.VMEM((2, slots, 2 * HEAD), BF16),
        xin=pltpu.VMEM(half, BF16),
        xg=pltpu.VMEM((rows, cols), BF16),
        send1=pltpu.VMEM((n_req, 16, qkv + 3 * HEAD), BF16),
        recv1=pltpu.VMEM((n_req, 16, qkv + 3 * HEAD), BF16),
        ext=pltpu.VMEM((16, 2 * HEAD), F32),
        q=pltpu.VMEM((HEADS, 16, HEAD), BF16),
        score=pltpu.VMEM((HEADS * 16, slots), F32),
        fscore=pltpu.VMEM((16, slots), F32),
        att=pltpu.VMEM((HEADS * 16, HEAD), F32),
        lse=pltpu.VMEM((HEADS * 16, HEAD), F32),
        mixed=pltpu.VMEM((n_req, 16, qw + 2 * HEAD), BF16),
        lhs=pltpu.VMEM((n_req, 16, qw), BF16),
        send3=pltpu.VMEM(half, BF16),
        recv3=pltpu.VMEM(half, BF16),
        res=pltpu.VMEM(half, BF16),
        hid0=pltpu.VMEM((n_req, 16, cuts[2] * HEAD), BF16),
        hid1=pltpu.VMEM((n_req, 16, (n - cuts[2]) * HEAD), BF16),
        down=pltpu.VMEM((rows, cols), F32),
        send7=pltpu.VMEM(half, BF16),
        recv7=pltpu.VMEM(half, BF16),
        oblk=pltpu.VMEM((2, blk, cols // 2), BF16),
        out=pltpu.VMEM(half, BF16),
        wsem=pltpu.SemaphoreType.DMA((8,)),
    )
    for g, (begin, end) in enumerate(ff_parts):
        wide = (end - begin) * 256 + (HEAD if g == 0 else 0)
        scratch[f"fs{g}"] = pltpu.VMEM((SIDE, SIDE, 16, wide), BF16)
        scratch[f"fr{g}"] = pltpu.VMEM((SIDE, SIDE, 16, wide), BF16)
        scratch[f"ft{g}"] = pltpu.VMEM((SIDE, 16, wide), BF16)
        scratch[f"fu{g}"] = pltpu.VMEM((SIDE, 16, wide), BF16)
    for name, count in dict(p1=1, p2=1, p3=2, p4=2, f1=4, f2=4, p6=2, p7=2, p8=2, **{"in": 2}, back=1).items():
        scratch["ss_" + name] = pltpu.SemaphoreType.DMA((count,))
        scratch["rs_" + name] = pltpu.SemaphoreType.DMA((count,))
    names = list(scratch)

    def body(*refs):
        plain, rest = refs[:13], refs[13:]
        kernel((n_req, n_head, cols * n_req), ff_parts, *plain, dict(zip(names, rest)))

    out = pl.pallas_call(
        body,
        out_shape=jax.ShapeDtypeStruct((n_head, blk, cols), BF16),
        in_specs=[smem, hbm, vmem, hbm, hbm, vmem, hbm, hbm, hbm, hbm, vmem, vmem],
        out_specs=vmem,
        scratch_shapes=[scratch[name] for name in names],
        compiler_params=pltpu.CompilerParams(
            collective_id=0, has_side_effects=True, vmem_limit_bytes=56 * 2**20
        ),
        name="two_layers",
    )(
        long_split.T,
        tokens.reshape(n_head, blk, cols),
        attention_gain,
        query_key_value_weight.reshape(cols, qkv),
        head_output_weight.reshape(qw, cols),
        feedforward_gain,
        gate_up.reshape(cols, 2, ff),
        down_weight.reshape(ff, cols),
        packed_cache.reshape(slots, 2 * HEAD),
        long_cache.reshape(2, slots, 2 * HEAD),
        lengths,
        inverse,
    )
    return out.reshape(1, rows, cols)


def solution(mesh):
    placed = (
        P(None, "req"),
        P("section", "req"),
        P("section", "req", "head", None),
        P("section", "head", None, "req"),
        P("section", "req"),
        P("section", "req", None, "head"),
        P("section", "head", "req"),
        P("section", "req", "head", None),
        P("section", None, "req", "head", None),
        P("req", None),
        P(None, "req"),
    )
    return jax.shard_map(
        local, mesh=mesh, in_specs=placed, out_specs=P("section", None, "req"), check_vma=False
    )
```

```python
import functools
import math

import jax
import jax.numpy as jnp
import numpy as np
from jax import lax
from jax.experimental import pallas as pl
from jax.experimental.pallas import tpu as pltpu
from jax.sharding import PartitionSpec as P

HEAD = 128
HEADS = 8
LONG = 16384
EPSILON = 1e-05
NEG = -1e30
F32 = jnp.float32
BF16 = jnp.bfloat16
MESH = pl.DeviceIdType.MESH
SIDE = 4
FAR_FIRST = sorted(
    ((a, b) for a in range(SIDE) for b in range(SIDE) if a or b),
    key=lambda d: (-(d[0] > 0) - (d[1] > 0), -min(d[0], SIDE - d[0]) - min(d[1], SIDE - d[1]), d),
)


def split_two(value, lanes):
    high = value.astype(BF16).astype(F32)
    return jnp.where(lanes < 64, high, value - high).astype(BF16)


def rope(block, table):
    swapped = jnp.concatenate([block[:, HEAD // 2 :], block[:, : HEAD // 2]], axis=1)
    return block * table[0] + swapped * table[1]


def rope_tables(position, inverse):
    angles = position * inverse
    lane = lax.broadcasted_iota(jnp.int32, angles.shape, 1)
    sine = jnp.sin(angles)
    return jnp.cos(angles), jnp.where(lane < HEAD // 2, -sine, sine)


def kernel(dims, ff_parts, split_ref, tok_hbm, gain1_ref, wqkv_hbm, wo_hbm, gain2_ref, raw_hbm, wd_hbm, pack_hbm, far_hbm,
           len_ref, inv_ref, out_ref, scratch):
    n_req, n_head, width = dims
    s = scratch
    sec = lax.axis_index("section")
    me = lax.axis_index("req")
    mz = lax.axis_index("head")
    mx, my = lax.div(me, SIDE), lax.rem(me, SIDE)
    xin = s["xin"]
    n_half, _, blk, hcols = xin.shape
    cols = n_half * hcols
    rows = n_head * blk
    slots = s["pack"].shape[0]
    qw = HEADS * HEAD
    ff = s["wd"].shape[0]
    scale = 1.0 / math.sqrt(HEAD)
    mid = n_req // 2
    ext_at = qw + 2 * HEAD
    stat_at = ext_at + HEAD

    def remote(source, target, name, where, peer):
        return pltpu.make_async_remote_copy(
            src_ref=source, dst_ref=target, send_sem=s["ss_" + name].at[where], recv_sem=s["rs_" + name].at[where],
            device_id=peer, device_id_type=MESH,
        )

    def req_peer(step):
        return {"req": lax.rem(mx + step[0], SIDE) * SIDE + lax.rem(my + step[1], SIDE)}

    ring = sorted(range(1, n_head), key=lambda k: (-min(k, n_head - k), k))

    def head_peer(k):
        return {"head": lax.rem(mz + k, n_head)}

    def spread_req(name, source, target, where=0):
        for step in FAR_FIRST:
            peer = req_peer(step)
            remote(source(peer["req"]), target.at[me], name, where, peer).start()

    def spread_head(name, source, target, where=0):
        for k in ring:
            peer = head_peer(k)
            remote(source(peer["head"]), target.at[mz], name, where, peer).start()

    def arrived(name, target, count, where=0):
        whole = target.at[pl.ds(0, count)]
        remote(whole, whole, name, where, {"section": 1 - sec}).wait_recv()

    def sent(name, source, count, where=0):
        whole = source.at[pl.ds(0, count)]
        remote(whole, whole, name, where, {"section": 1 - sec}).wait_send()

    def load(source, target, n):
        return pltpu.make_async_copy(source, target, s["wsem"].at[n])

    load_qkv = load(wqkv_hbm, s["wqkv"], 0)
    load_raw = load(raw_hbm, s["raw"], 1)
    load_pack = load(pack_hbm, s["pack"], 2)
    load_far = load(far_hbm, s["far"], 3)
    load_wo = load(wo_hbm, s["wo"], 4)
    load_wd = load(wd_hbm, s["wd"], 5)
    load_qkv.start()

    @pl.when(sec == 0)
    def _():
        for h in range(n_half):
            load(tok_hbm.at[:, :, pl.ds(h * hcols, hcols)], xin.at[h], 6 + h).start()

    barrier = pltpu.get_barrier_semaphore()

    for step in FAR_FIRST:
        pl.semaphore_signal(barrier, inc=1, device_id=req_peer(step), device_id_type=MESH)
    for k in ring:
        pl.semaphore_signal(barrier, inc=1, device_id=head_peer(k), device_id_type=MESH)
    for k in ring + [0]:
        pl.semaphore_signal(barrier, inc=1, device_id={"section": 1 - sec, **head_peer(k)}, device_id_type=MESH)

    for other in (load_raw, load_pack, load_far, load_wo, load_wd):
        other.start()

    def lane_sum(mask, shape):
        lens = jnp.broadcast_to(len_ref[...].astype(F32), shape)
        return jnp.sum(jnp.where(mask, lens, 0.0), axis=1, keepdims=True)

    r16 = lax.broadcasted_iota(jnp.int32, (16, 16), 0)
    k16 = lax.broadcasted_iota(jnp.int32, (16, 16), 1)
    is_long = (lax.broadcasted_iota(jnp.int32, (16, 1), 0) == 0) & ((me == 0) | (me == mid))
    position = lane_sum(k16 == r16, (16, 16)) + jnp.where(is_long, float(LONG), 0.0)

    lanes = lax.broadcasted_iota(jnp.int32, (rows, HEAD), 1)
    lane16 = lax.broadcasted_iota(jnp.int32, (16, HEAD), 1)

    def normed(source, gain_ref):
        squares = jnp.zeros((rows, 1), F32)
        for h in range(n_half):
            at = pl.ds(h * hcols, hcols)
            x = source[h].reshape(rows, hcols).astype(F32)
            squares = squares + jnp.sum(x * x, axis=1, keepdims=True)
            s["xg"][:, at] = (x * gain_ref[:, at].astype(F32)).astype(BF16)
        return squares

    def first_products():
        squares = normed(xin, gain1_ref)
        load_qkv.wait()

        @pl.loop(0, ext_at // 256)
        def _(c):
            at = pl.ds(pl.multiple_of(c * 256, 256), 256)
            part = jnp.dot(s["xg"][...], s["wqkv"][:, at], preferred_element_type=F32)
            s["send1"][:, :, at] = part.astype(BF16).reshape(n_req, 16, 256)

        ext = s["ext"]
        for j in range(2):
            row = s["send1"][j * mid, :, 0:qw].astype(F32)[0:1]
            for h in range(HEADS):
                ext[j * 8 + h : j * 8 + h + 1, :] = row[:, h * HEAD : (h + 1) * HEAD]
        head = ext[...].astype(BF16)
        first = position[0:1]
        upper = jnp.floor(first * (1.0 / 256.0))
        lower = first - 256.0 * upper
        row16 = lax.broadcasted_iota(jnp.int32, (16, HEAD), 0)
        far_squares = jnp.where(row16 < 8, squares[0:1], squares[mid * 16 : mid * 16 + 1])
        far_high = far_squares.astype(BF16).astype(F32)
        common = jnp.where(
            lane16 < 80, far_high, jnp.where(lane16 < 96, far_squares - far_high, jnp.where(lane16 < 112, upper, lower))
        )
        high = squares.astype(BF16).astype(F32)
        pair = jnp.where(lanes < 32, high, squares - high).reshape(n_req, 16, HEAD)
        for g in range(n_req):
            s["send1"][g, :, ext_at : ext_at + HEAD] = head
            s["send1"][g, :, stat_at : stat_at + HEAD] = jnp.where(lane16 < 64, pair[g], common).astype(BF16)

    def split_gate():
        load_raw.wait()
        raw, wgu = s["raw"], s["wgu"]

        @pl.loop(0, cols // 16)
        def _(k):
            at = pl.ds(pl.multiple_of(k * 16, 16), 16)
            for c in range(ff // HEAD):
                source = pl.ds(c * HEAD, HEAD)
                wgu[at, pl.ds(c * 256, HEAD)] = raw[at, 0, source]
                wgu[at, pl.ds(c * 256 + HEAD, HEAD)] = raw[at, 1, source]

    @pl.when(sec == 0)
    def _():
        for h in range(n_half):
            load(tok_hbm.at[:, :, pl.ds(h * hcols, hcols)], xin.at[h], 6 + h).wait()
        first_products()

    pl.semaphore_wait(barrier, n_req - 1 + n_head - 1 + n_head)

    @pl.when(sec == 1)
    def _():
        split_gate()
        for h in range(n_half):
            remote(xin.at[h], xin.at[h], "in", h, {"section": 0}).wait_recv()
        remote(xin, s["out"], "back", 0, {"section": 0}).start()
        first_products()

    spread_req("p1", lambda p: s["send1"].at[p], s["recv1"])
    s["recv1"][me] = s["send1"][me]

    @pl.when(sec == 0)
    def _():
        split_gate()

    own_table = rope_tables(position, inv_ref[...])
    r_id = lax.broadcasted_iota(jnp.int32, (16 * HEADS, 16), 0) & 15
    k_id = lax.broadcasted_iota(jnp.int32, (16 * HEADS, 16), 1)
    seg_end = lane_sum(k_id <= r_id, (16 * HEADS, 16)).astype(jnp.int32)
    seg_start = lane_sum(k_id < r_id, (16 * HEADS, 16)).astype(jnp.int32)
    load_pack.wait()
    load_far.wait()
    pack, far = s["pack"], s["far"]
    recv1 = s["recv1"]
    arrived("p1", recv1, n_req - 1)

    def total_of(ref, at):
        value = ref[0, :, at].astype(F32)
        for p in range(1, ref.shape[0]):
            value = value + ref[p, :, at].astype(F32)
        return value

    stat = total_of(recv1, pl.ds(stat_at, HEAD))
    row_scale = lax.rsqrt((stat[:, 0:1] + stat[:, 32:33]) / width + EPSILON)

    @pl.loop(0, HEADS)
    def _(h):
        at = pl.ds(pl.multiple_of(h * HEAD, HEAD), HEAD)
        s["q"][h] = rope(total_of(recv1, at) * row_scale, own_table).astype(BF16)

    new_key = rope(total_of(recv1, pl.ds(qw, HEAD)) * row_scale, own_table).astype(BF16)
    new_value = (total_of(recv1, pl.ds(qw + HEAD, HEAD)) * row_scale).astype(BF16)
    queries = s["q"][...].reshape(HEADS * 16, HEAD)
    keys = jnp.concatenate([new_key.astype(F32)] * HEADS, axis=0)
    values = jnp.concatenate([new_value.astype(F32)] * HEADS, axis=0)
    own = jnp.sum(queries.astype(F32) * keys, axis=1, keepdims=True) * scale

    total = total_of(recv1, pl.ds(ext_at, HEAD))
    far_scale = lax.rsqrt((stat[:, 64:65] + stat[:, 80:81]) / width + EPSILON)
    low8 = lax.broadcasted_iota(jnp.int32, (16, HEAD), 0) < 8
    places = jnp.where(
        low8, recv1[0, :, stat_at : stat_at + HEAD].astype(F32), recv1[mid, :, stat_at : stat_at + HEAD].astype(F32)
    )
    far_table = rope_tables(places[:, 96:97] * 256.0 + places[:, 112:113], inv_ref[...])
    far_query = rope(total * far_scale, far_table).astype(BF16)

    chunk = min(512, slots)
    n_chunk = slots // chunk
    contract = (((1,), (1,)), ((), ()))
    low_chunk = lax.broadcasted_iota(jnp.int32, (16, chunk), 0) < 8
    live = jnp.where(low_chunk, split_ref[0, 0], split_ref[0, 1])

    def scores_of(c, best):
        far_best, near_best = best
        at = pl.ds(pl.multiple_of(c * chunk, chunk), chunk)
        a = lax.dot_general(far_query, far[0, at, 0:HEAD], contract, preferred_element_type=F32)
        b = lax.dot_general(far_query, far[1, at, 0:HEAD], contract, preferred_element_type=F32)
        slot = lax.broadcasted_iota(jnp.int32, (16, chunk), 1) + c * chunk
        value = jnp.where(slot < live, jnp.where(low_chunk, a, b) * scale, NEG)
        s["fscore"][:, at] = value
        far_best = jnp.maximum(far_best, jnp.max(value, axis=1, keepdims=True))
        near = lax.dot_general(queries, pack[at, 0:HEAD], contract, preferred_element_type=F32)
        slot = lax.broadcasted_iota(jnp.int32, (HEADS * 16, chunk), 1) + c * chunk
        value = jnp.where((slot >= seg_start) & (slot < seg_end), near * scale, NEG)
        s["score"][:, at] = value
        return far_best, jnp.maximum(near_best, jnp.max(value, axis=1, keepdims=True))

    far_max, row_max = lax.fori_loop(0, n_chunk, scores_of, (jnp.full((16, 1), NEG, F32), own))
    own_weight = jnp.exp(own - row_max).astype(BF16).astype(F32)

    def sums_of(c, carry):
        far_totals, far_sum, totals, summed = carry
        at = pl.ds(pl.multiple_of(c * chunk, chunk), chunk)
        w = jnp.exp(s["fscore"][:, at] - far_max).astype(BF16)
        a = jnp.dot(w, far[0, at, HEAD:], preferred_element_type=F32)
        b = jnp.dot(w, far[1, at, HEAD:], preferred_element_type=F32)
        far_totals = far_totals + jnp.sum(w.astype(F32), axis=1, keepdims=True)
        far_sum = far_sum + jnp.where(low8, a, b)
        w = jnp.exp(s["score"][:, at] - row_max).astype(BF16)
        summed = summed + jnp.dot(w, pack[at, HEAD:], preferred_element_type=F32)
        return far_totals, far_sum, totals + jnp.sum(w.astype(F32), axis=1, keepdims=True), summed

    far_totals, far_sum, totals, summed = lax.fori_loop(
        0, n_chunk, sums_of,
        (jnp.zeros((16, 1), F32), jnp.zeros((16, HEAD), F32), own_weight, own_weight * values),
    )
    far_out = far_sum / far_totals
    far_lse = jnp.broadcast_to(far_max + jnp.log(far_totals), (16, HEAD))
    attended = summed / totals
    s["att"][...] = attended
    s["lse"][...] = jnp.broadcast_to(row_max + jnp.log(totals), (HEADS * 16, HEAD))
    mixed = s["mixed"]
    for h in range(HEADS):
        mixed[me, :, h * HEAD : (h + 1) * HEAD] = attended[h * 16 : (h + 1) * 16].astype(BF16)

    first_out = s["att"][pl.ds(0, HEADS, stride=16), :]
    first_lse = s["lse"][pl.ds(0, HEADS, stride=16), :]
    near_out = jnp.concatenate([first_out, first_out], axis=0)
    near_lse = jnp.concatenate([first_lse, first_lse], axis=0)
    owned = jnp.where(low8, 0, mid) == me
    peak = jnp.maximum(far_lse, near_lse)
    fa = jnp.exp(far_lse - peak)
    na = jnp.exp(near_lse - peak)
    part_out = jnp.where(owned, (fa * far_out + na * near_out) / (fa + na), far_out)
    part_lse = jnp.where(owned, peak + jnp.log(fa + na), far_lse)
    high = part_lse.astype(BF16).astype(F32)
    middle = (part_lse - high).astype(BF16).astype(F32)
    low = part_lse - high - middle
    mixed[me, :, qw : qw + HEAD] = part_out.astype(BF16)
    mixed[me, :, qw + HEAD :] = jnp.where(lane16 < 32, high, jnp.where(lane16 < 64, middle, low)).astype(BF16)
    spread_req("p2", lambda p: mixed.at[me], mixed)
    sent("p1", s["send1"], n_req - 1)
    load_wo.wait()
    arrived("p2", mixed, n_req - 1)

    parts = []
    for p in range(n_req):
        part = mixed[p, :, qw + HEAD :].astype(F32)
        parts.append(part[:, 0:1] + part[:, 32:33] + part[:, 64:65])
    peak = functools.reduce(jnp.maximum, parts)
    den = jnp.zeros((16, 1), F32)
    num = jnp.zeros((16, HEAD), F32)
    for p in range(n_req):
        w = jnp.exp(parts[p] - peak)
        den = den + w
        num = num + w * mixed[p, :, qw : qw + HEAD].astype(F32)
    long_out = num / den
    lhs = s["lhs"]
    lhs[...] = mixed[:, :, 0:qw]
    first = lax.broadcasted_iota(jnp.int32, (16, qw), 0) == 0
    for j in range(2):
        flat = jnp.concatenate([long_out[j * 8 + h : j * 8 + h + 1] for h in range(HEADS)], axis=1)
        block = mixed[j * mid, :, 0:qw].astype(F32)
        lhs[j * mid] = jnp.where(first, jnp.broadcast_to(flat, (16, qw)), block).astype(BF16)

    send3, recv3, res = s["send3"], s["recv3"], s["res"]
    for h in range(n_half):
        part = jnp.dot(lhs[...].reshape(rows, qw), s["wo"][:, pl.ds(h * hcols, hcols)], preferred_element_type=F32)
        send3[h] = part.astype(BF16).reshape(n_head, blk, hcols)
        spread_head("p3", lambda p, h=h: send3.at[h, p], recv3.at[h], h)
    sent("p2", mixed, n_req - 1)

    def block_total(buffer, mine, h):
        value = mine[h, mz].astype(F32)
        for k in range(1, n_head):
            value = value + buffer[h, lax.rem(mz + k, n_head)].astype(F32)
        return value

    for h in range(n_half):
        arrived("p3", recv3.at[h], n_head - 1, h)
        res[h, mz] = (xin[h, mz].astype(F32) + block_total(recv3, send3, h)).astype(BF16)
        spread_head("p4", lambda p, h=h: res.at[h, mz], res.at[h], h)
    for h in range(n_half):
        sent("p3", send3.at[h], n_head - 1, h)
    for h in range(n_half):
        arrived("p4", res.at[h], n_head - 1, h)

    squares = normed(res, gain2_ref)
    n_part = len(ff_parts)

    def along(side, k):
        if side == 0:
            c = lax.rem(mx + k, SIDE)
            return c, {"req": c * SIDE + my}
        c = lax.rem(my + k, SIDE)
        return c, {"req": mx * SIDE + c}

    coordinate = (mx, my)
    for g, (begin, end) in enumerate(ff_parts):
        buf = s[f"fs{g}"]

        @pl.loop(begin, end)
        def _(c, g=g, buf=buf, begin=begin):
            part = jnp.dot(
                s["xg"][...], s["wgu"][:, pl.ds(pl.multiple_of(c * 256, 256), 256)], preferred_element_type=F32
            ).astype(BF16).reshape(SIDE, SIDE, 16, 256)
            at = pl.ds(pl.multiple_of((c - begin) * 256, 256), 256)
            for a in range(SIDE):
                if g % 2 == 0:
                    buf[a, :, :, at] = part[a]
                else:
                    buf[a, :, :, at] = part[:, a]

        if g == 0:
            at = pl.ds((end - begin) * 256, HEAD)
            buf[:, :, :, at] = split_two(squares, lanes).reshape(SIDE, SIDE, 16, HEAD)
        for k in range(1, SIDE):
            c, peer = along(g % 2, k)
            remote(buf.at[c], s[f"fr{g}"].at[coordinate[g % 2]], "f1", g, peer).start()
    for h in range(n_half):
        sent("p4", res.at[h], n_head - 1, h)

    for g, (begin, end) in enumerate(ff_parts):
        side = g % 2
        buf, got, turn = s[f"fs{g}"], s[f"fr{g}"], s[f"ft{g}"]
        arrived("f1", got, SIDE - 1, g)
        mine = coordinate[side]

        @pl.loop(0, SIDE)
        def _(b, g=g, buf=buf, got=got, turn=turn, mine=mine, begin=begin, end=end):
            value = buf[mine, b].astype(F32)
            for k in range(1, SIDE):
                value = value + got[lax.rem(mine + k, SIDE), b].astype(F32)
            turn[b] = value.astype(BF16)
            if g == 0:
                stat = value[:, (end - begin) * 256 :]
                turn[b, :, pl.ds((end - begin) * 256, HEAD)] = split_two(stat[:, 0:1] + stat[:, 64:65], lane16)

        for k in range(1, SIDE):
            c, peer = along(1 - side, k)
            remote(turn.at[c], s[f"fu{g}"].at[coordinate[1 - side]], "f2", g, peer).start()

    ff_scale = None
    hid = (s["hid0"], s["hid1"])
    for g, (begin, end) in enumerate(ff_parts):
        side = g % 2
        turn, got = s[f"ft{g}"], s[f"fu{g}"]
        arrived("f2", got, SIDE - 1, g)
        mine = coordinate[1 - side]

        def turned(at, turn=turn, got=got, mine=mine):
            value = turn[mine, :, at].astype(F32)
            for k in range(1, SIDE):
                value = value + got[lax.rem(mine + k, SIDE), :, at].astype(F32)
            return value

        if g == 0:
            stat = turned(pl.ds((end - begin) * 256, HEAD))
            ff_scale = lax.rsqrt((stat[:, 0:1] + stat[:, 64:65]) / width + EPSILON)
        which = g // 2
        base = ff_parts[2 * which][0]
        for c in range(begin, end):
            both = turned(pl.ds((c - begin) * 256, 256)) * ff_scale
            gate, up = both[:, :HEAD], both[:, HEAD:]
            hid[which][me, :, pl.ds((c - base) * HEAD, HEAD)] = (gate / (1.0 + jnp.exp(-gate)) * up).astype(BF16)
        if g % 2 == 1:
            spread_req("p6", lambda p, which=which: hid[which].at[me], hid[which], which)
    for g in range(n_part):
        sent("f1", s[f"fs{g}"], SIDE - 1, g)
        sent("f2", s[f"ft{g}"], SIDE - 1, g)

    load_wd.wait()
    send7, recv7, oblk, out, down = s["send7"], s["recv7"], s["oblk"], s["out"], s["down"]
    wide0 = hid[0].shape[2]
    arrived("p6", hid[0], n_req - 1, 0)
    for h in range(n_half):
        at = pl.ds(h * hcols, hcols)
        down[:, at] = jnp.dot(hid[0][...].reshape(rows, wide0), s["wd"][pl.ds(0, wide0), at], preferred_element_type=F32)
    arrived("p6", hid[1], n_req - 1, 1)
    for h in range(n_half):
        at = pl.ds(h * hcols, hcols)
        part = down[:, at] + jnp.dot(
            hid[1][...].reshape(rows, ff - wide0), s["wd"][pl.ds(wide0, ff - wide0), at], preferred_element_type=F32
        )
        send7[h] = part.astype(BF16).reshape(n_head, blk, hcols)
        spread_head("p7", lambda p, h=h: send7.at[h, p], recv7.at[h], h)
    for which in range(2):
        sent("p6", hid[which], n_req - 1, which)

    def hand_over(k, h):
        return remote(oblk.at[h], xin.at[h, mz], "in", h, {"section": 1, **head_peer(k)})

    for h in range(n_half):
        arrived("p7", recv7.at[h], n_head - 1, h)
        oblk[h] = (res[h, mz].astype(F32) + block_total(recv7, send7, h)).astype(BF16)

        @pl.when(sec == 0)
        def _(h=h):
            for k in ring + [0]:
                hand_over(k, h).start()

        @pl.when(sec == 1)
        def _(h=h):
            out[h, mz] = oblk[h]
            spread_head("p8", lambda p: oblk.at[h], out.at[h], h)

    for h in range(n_half):
        sent("p7", send7.at[h], n_head - 1, h)

    @pl.when(sec == 0)
    def _():
        remote(xin, out, "back", 0, {"section": 1}).wait_recv()
        for h in range(n_half):
            remote(xin.at[h], xin.at[h], "in", h, {"section": 1}).wait_send()

    @pl.when(sec == 1)
    def _():
        for h in range(n_half):
            arrived("p8", out.at[h], n_head - 1, h)

    for h in range(n_half):
        out_ref[:, :, pl.ds(h * hcols, hcols)] = out[h]

    @pl.when(sec == 1)
    def _():
        for h in range(n_half):
            sent("p8", out.at[h], n_head - 1, h)
        remote(xin, out, "back", 0, {"section": 0}).wait_send()


def local(
    tokens,
    attention_gain,
    query_key_value_weight,
    head_output_weight,
    feedforward_gain,
    gate_up,
    down_weight,
    packed_cache,
    long_cache,
    lengths,
    long_split,
):
    n_req = lax.axis_size("req")
    n_head = lax.axis_size("head")
    rows, cols = tokens.shape
    blk = rows // n_head
    qkv = query_key_value_weight.shape[3]
    qw = head_output_weight.shape[2]
    ff = down_weight.shape[1]
    slots = packed_cache.shape[1]
    assert slots == long_cache.shape[2] and rows == n_req * 16 and n_req == SIDE * SIDE
    half = (2, n_head, blk, cols // 2)
    n = ff // HEAD
    cuts = (0, 3 * n // 14, 6 * n // 14, 10 * n // 14, n)
    ff_parts = tuple(zip(cuts[:-1], cuts[1:]))
    freq_ids = np.arange(HEAD // 2, dtype=np.float32)
    inverse = np.float32(1.0) / np.power(np.float32(10000.0), freq_ids * np.float32(2.0) / np.float32(HEAD))
    inverse = jnp.asarray(np.concatenate([inverse, inverse])[None].astype(np.float32))
    vmem = pl.BlockSpec(memory_space=pltpu.VMEM)
    hbm = pl.BlockSpec(memory_space=pl.ANY)
    smem = pl.BlockSpec(memory_space=pltpu.SMEM)
    scratch = dict(
        wqkv=pltpu.VMEM((cols, qkv), BF16),
        wo=pltpu.VMEM((qw, cols), BF16),
        raw=pltpu.VMEM((cols, 2, ff), BF16),
        wgu=pltpu.VMEM((cols, 2 * ff), BF16),
        wd=pltpu.VMEM((ff, cols), BF16),
        pack=pltpu.VMEM((slots, 2 * HEAD), BF16),
        far=pltpu.VMEM((2, slots, 2 * HEAD), BF16),
        xin=pltpu.VMEM(half, BF16),
        xg=pltpu.VMEM((rows, cols), BF16),
        send1=pltpu.VMEM((n_req, 16, qkv + 2 * HEAD), BF16),
        recv1=pltpu.VMEM((n_req, 16, qkv + 2 * HEAD), BF16),
        ext=pltpu.VMEM((16, HEAD), F32),
        q=pltpu.VMEM((HEADS, 16, HEAD), BF16),
        score=pltpu.VMEM((HEADS * 16, slots), F32),
        fscore=pltpu.VMEM((16, slots), F32),
        att=pltpu.VMEM((HEADS * 16, HEAD), F32),
        lse=pltpu.VMEM((HEADS * 16, HEAD), F32),
        mixed=pltpu.VMEM((n_req, 16, qw + 2 * HEAD), BF16),
        lhs=pltpu.VMEM((n_req, 16, qw), BF16),
        send3=pltpu.VMEM(half, BF16),
        recv3=pltpu.VMEM(half, BF16),
        res=pltpu.VMEM(half, BF16),
        hid0=pltpu.VMEM((n_req, 16, cuts[2] * HEAD), BF16),
        hid1=pltpu.VMEM((n_req, 16, (n - cuts[2]) * HEAD), BF16),
        down=pltpu.VMEM((rows, cols), F32),
        send7=pltpu.VMEM(half, BF16),
        recv7=pltpu.VMEM(half, BF16),
        oblk=pltpu.VMEM((2, blk, cols // 2), BF16),
        out=pltpu.VMEM(half, BF16),
        wsem=pltpu.SemaphoreType.DMA((8,)),
    )
    for g, (begin, end) in enumerate(ff_parts):
        wide = (end - begin) * 256 + (HEAD if g == 0 else 0)
        scratch[f"fs{g}"] = pltpu.VMEM((SIDE, SIDE, 16, wide), BF16)
        scratch[f"fr{g}"] = pltpu.VMEM((SIDE, SIDE, 16, wide), BF16)
        scratch[f"ft{g}"] = pltpu.VMEM((SIDE, 16, wide), BF16)
        scratch[f"fu{g}"] = pltpu.VMEM((SIDE, 16, wide), BF16)
    for name, count in dict(p1=1, p2=1, p3=2, p4=2, f1=4, f2=4, p6=2, p7=2, p8=2, **{"in": 2}, back=1).items():
        scratch["ss_" + name] = pltpu.SemaphoreType.DMA((count,))
        scratch["rs_" + name] = pltpu.SemaphoreType.DMA((count,))
    names = list(scratch)

    def body(*refs):
        plain, rest = refs[:13], refs[13:]
        kernel((n_req, n_head, cols * n_req), ff_parts, *plain, dict(zip(names, rest)))

    out = pl.pallas_call(
        body,
        out_shape=jax.ShapeDtypeStruct((n_head, blk, cols), BF16),
        in_specs=[smem, hbm, vmem, hbm, hbm, vmem, hbm, hbm, hbm, hbm, vmem, vmem],
        out_specs=vmem,
        scratch_shapes=[scratch[name] for name in names],
        compiler_params=pltpu.CompilerParams(
            collective_id=0, has_side_effects=True, vmem_limit_bytes=56 * 2**20
        ),
        name="two_layers",
    )(
        long_split.T,
        tokens.reshape(n_head, blk, cols),
        attention_gain,
        query_key_value_weight.reshape(cols, qkv),
        head_output_weight.reshape(qw, cols),
        feedforward_gain,
        gate_up.reshape(cols, 2, ff),
        down_weight.reshape(ff, cols),
        packed_cache.reshape(slots, 2 * HEAD),
        long_cache.reshape(2, slots, 2 * HEAD),
        lengths,
        inverse,
    )
    return out.reshape(1, rows, cols)


def solution(mesh):
    placed = (
        P(None, "req"),
        P("section", "req"),
        P("section", "req", "head", None),
        P("section", "head", None, "req"),
        P("section", "req"),
        P("section", "req", None, "head"),
        P("section", "head", "req"),
        P("section", "req", "head", None),
        P("section", None, "req", "head", None),
        P("req", None),
        P(None, "req"),
    )
    return jax.shard_map(
        local, mesh=mesh, in_specs=placed, out_specs=P("section", None, "req"), check_vma=False
    )
```

```python
import functools
import math

import jax
import jax.numpy as jnp
import numpy as np
from jax import lax
from jax.experimental import pallas as pl
from jax.experimental.pallas import tpu as pltpu
from jax.sharding import PartitionSpec as P

HEAD = 128
HEADS = 8
LONG = 16384
EPSILON = 1e-05
NEG = -1e30
F32 = jnp.float32
BF16 = jnp.bfloat16
MESH = pl.DeviceIdType.MESH
SIDE = 4
FAR_FIRST = sorted(
    ((a, b) for a in range(SIDE) for b in range(SIDE) if a or b),
    key=lambda d: (-(d[0] > 0) - (d[1] > 0), -min(d[0], SIDE - d[0]) - min(d[1], SIDE - d[1]), d),
)


PIECES = 2
PARTS = (1, 1, 2, 2, 2, 2, 2, 2)
SETS = ((0, 1, 2, 3), (4, 5), (6, 7))


def split_two(value, lanes):
    high = value.astype(BF16).astype(F32)
    return jnp.where(lanes < 64, high, value - high).astype(BF16)


def rope(block, table):
    swapped = jnp.concatenate([block[:, HEAD // 2 :], block[:, : HEAD // 2]], axis=1)
    return block * table[0] + swapped * table[1]


def rope_tables(position, inverse):
    angles = position * inverse
    lane = lax.broadcasted_iota(jnp.int32, angles.shape, 1)
    sine = jnp.sin(angles)
    return jnp.cos(angles), jnp.where(lane < HEAD // 2, -sine, sine)


def kernel(dims, ff_parts, wides, split_ref, tok_hbm, gain1_ref, wqkv_hbm, wo_hbm, gain2_ref, raw_hbm, wd_hbm, pack_hbm, far_hbm,
           len_ref, inv_ref, out_ref, scratch):
    n_req, n_head, width = dims
    s = scratch
    sec = lax.axis_index("section")
    me = lax.axis_index("req")
    mz = lax.axis_index("head")
    mx, my = lax.div(me, SIDE), lax.rem(me, SIDE)
    xin = s["xin"]
    n_half, _, blk, hcols = xin.shape
    cols = n_half * hcols
    rows = n_head * blk
    slots = s["pack"].shape[0]
    qw = HEADS * HEAD
    ff = s["wd"].shape[0]
    scale = 1.0 / math.sqrt(HEAD)
    mid = n_req // 2
    ext_at = qw + 2 * HEAD
    stat_at = ext_at + HEAD

    def remote(source, target, name, where, peer):
        return pltpu.make_async_remote_copy(
            src_ref=source, dst_ref=target, send_sem=s["ss_" + name].at[where], recv_sem=s["rs_" + name].at[where],
            device_id=peer, device_id_type=MESH,
        )

    def req_peer(step):
        return {"req": lax.rem(mx + step[0], SIDE) * SIDE + lax.rem(my + step[1], SIDE)}

    ring = sorted(range(1, n_head), key=lambda k: (-min(k, n_head - k), k))

    def head_peer(k):
        return {"head": lax.rem(mz + k, n_head)}

    def spread_req(name, source, target, where=0):
        for step in FAR_FIRST:
            peer = req_peer(step)
            remote(source(peer["req"]), target.at[me], name, where, peer).start()

    def spread_head(name, source, target, where=0):
        for k in ring:
            peer = head_peer(k)
            remote(source(peer["head"]), target.at[mz], name, where, peer).start()

    def arrived(name, target, count, where=0):
        whole = target.at[pl.ds(0, count)]
        remote(whole, whole, name, where, {"section": 1 - sec}).wait_recv()

    def sent(name, source, count, where=0):
        whole = source.at[pl.ds(0, count)]
        remote(whole, whole, name, where, {"section": 1 - sec}).wait_send()

    def load(source, target, n):
        return pltpu.make_async_copy(source, target, s["wsem"].at[n])

    load_qkv = load(wqkv_hbm, s["wqkv"], 0)
    load_raw = load(raw_hbm, s["raw"], 1)
    load_pack = load(pack_hbm, s["pack"], 2)
    load_far = load(far_hbm, s["far"], 3)
    load_wo = load(wo_hbm, s["wo"], 4)
    load_wd = load(wd_hbm, s["wd"], 5)
    load_qkv.start()

    @pl.when(sec == 0)
    def _():
        for h in range(n_half):
            load(tok_hbm.at[:, :, pl.ds(h * hcols, hcols)], xin.at[h], 6 + h).start()

    barrier = pltpu.get_barrier_semaphore()

    def greet_section():
        for k in ring + [0]:
            pl.semaphore_signal(barrier, inc=1, device_id={"section": 1 - sec, **head_peer(k)}, device_id_type=MESH)

    pl.when(sec == 1)(greet_section)
    for step in FAR_FIRST:
        pl.semaphore_signal(barrier, inc=1, device_id=req_peer(step), device_id_type=MESH)
    for k in ring:
        pl.semaphore_signal(barrier, inc=1, device_id=head_peer(k), device_id_type=MESH)
    pl.when(sec == 0)(greet_section)

    for other in (load_raw, load_pack, load_far, load_wo, load_wd):
        other.start()

    def lane_sum(mask, shape):
        lens = jnp.broadcast_to(len_ref[...].astype(F32), shape)
        return jnp.sum(jnp.where(mask, lens, 0.0), axis=1, keepdims=True)

    r16 = lax.broadcasted_iota(jnp.int32, (16, 16), 0)
    k16 = lax.broadcasted_iota(jnp.int32, (16, 16), 1)
    is_long = (lax.broadcasted_iota(jnp.int32, (16, 1), 0) == 0) & ((me == 0) | (me == mid))
    position = lane_sum(k16 == r16, (16, 16)) + jnp.where(is_long, float(LONG), 0.0)

    lanes = lax.broadcasted_iota(jnp.int32, (rows, HEAD), 1)
    lane16 = lax.broadcasted_iota(jnp.int32, (16, HEAD), 1)

    def normed(source, gain_ref):
        squares = jnp.zeros((rows, 1), F32)
        for h in range(n_half):
            at = pl.ds(h * hcols, hcols)
            x = source[h].reshape(rows, hcols).astype(F32)
            squares = squares + jnp.sum(x * x, axis=1, keepdims=True)
            s["xg"][:, at] = (x * gain_ref[:, at].astype(F32)).astype(BF16)
        return squares

    def first_products():
        squares = normed(xin, gain1_ref)
        load_qkv.wait()

        @pl.loop(0, ext_at // 256, unroll=True)
        def _(c):
            at = pl.ds(pl.multiple_of(c * 256, 256), 256)
            part = jnp.dot(s["xg"][...], s["wqkv"][:, at], preferred_element_type=F32)
            s["send1"][:, :, at] = part.astype(BF16).reshape(n_req, 16, 256)

        ext = s["ext"]
        for j in range(2):
            row = s["send1"][j * mid, :, 0:qw].astype(F32)[0:1]
            for h in range(HEADS):
                ext[j * 8 + h : j * 8 + h + 1, :] = row[:, h * HEAD : (h + 1) * HEAD]
        head = ext[...].astype(BF16)
        first = position[0:1]
        upper = jnp.floor(first * (1.0 / 256.0))
        lower = first - 256.0 * upper
        row16 = lax.broadcasted_iota(jnp.int32, (16, HEAD), 0)
        far_squares = jnp.where(row16 < 8, squares[0:1], squares[mid * 16 : mid * 16 + 1])
        far_high = far_squares.astype(BF16).astype(F32)
        common = jnp.where(
            lane16 < 80, far_high, jnp.where(lane16 < 96, far_squares - far_high, jnp.where(lane16 < 112, upper, lower))
        )
        high = squares.astype(BF16).astype(F32)
        pair = jnp.where(lanes < 32, high, squares - high).reshape(n_req, 16, HEAD)
        for g in range(n_req):
            s["send1"][g, :, ext_at : ext_at + HEAD] = head
            s["send1"][g, :, stat_at : stat_at + HEAD] = jnp.where(lane16 < 64, pair[g], common).astype(BF16)

    def split_gate():
        load_raw.wait()
        raw, wgu = s["raw"], s["wgu"]

        @pl.loop(0, cols // 16)
        def _(k):
            at = pl.ds(pl.multiple_of(k * 16, 16), 16)
            for c in range(ff // HEAD):
                source = pl.ds(c * HEAD, HEAD)
                wgu[at, pl.ds(c * 256, HEAD)] = raw[at, 0, source]
                wgu[at, pl.ds(c * 256 + HEAD, HEAD)] = raw[at, 1, source]

    @pl.when(sec == 0)
    def _():
        for h in range(n_half):
            load(tok_hbm.at[:, :, pl.ds(h * hcols, hcols)], xin.at[h], 6 + h).wait()
        first_products()

    pl.semaphore_wait(barrier, n_req - 1 + n_head - 1 + n_head)

    @pl.when(sec == 1)
    def _():
        split_gate()
        for h in range(n_half):
            remote(xin.at[h], xin.at[h], "in", h, {"section": 0}).wait_recv()
        remote(xin, s["out"], "back", 0, {"section": 0}).start()
        first_products()

    spread_req("p1", lambda p: s["send1"].at[p], s["recv1"])
    s["recv1"][me] = s["send1"][me]

    @pl.when(sec == 0)
    def _():
        split_gate()

    own_table = rope_tables(position, inv_ref[...])
    r_id = lax.broadcasted_iota(jnp.int32, (16 * HEADS, 16), 0) & 15
    k_id = lax.broadcasted_iota(jnp.int32, (16 * HEADS, 16), 1)
    seg_end = lane_sum(k_id <= r_id, (16 * HEADS, 16)).astype(jnp.int32)
    seg_start = lane_sum(k_id < r_id, (16 * HEADS, 16)).astype(jnp.int32)
    load_pack.wait()
    load_far.wait()
    pack, far = s["pack"], s["far"]
    recv1 = s["recv1"]
    arrived("p1", recv1, n_req - 1)

    def total_of(ref, at):
        value = ref[0, :, at].astype(F32)
        for p in range(1, ref.shape[0]):
            value = value + ref[p, :, at].astype(F32)
        return value

    stat = total_of(recv1, pl.ds(stat_at, HEAD))
    row_scale = lax.rsqrt((stat[:, 0:1] + stat[:, 32:33]) / width + EPSILON)

    for h in range(HEADS):
        at = pl.ds(h * HEAD, HEAD)
        s["q"][h] = rope(total_of(recv1, at) * row_scale, own_table).astype(BF16)

    new_key = rope(total_of(recv1, pl.ds(qw, HEAD)) * row_scale, own_table).astype(BF16)
    new_value = (total_of(recv1, pl.ds(qw + HEAD, HEAD)) * row_scale).astype(BF16)
    queries = s["q"][...].reshape(HEADS * 16, HEAD)
    keys = jnp.concatenate([new_key.astype(F32)] * HEADS, axis=0)
    values = jnp.concatenate([new_value.astype(F32)] * HEADS, axis=0)
    own = jnp.sum(queries.astype(F32) * keys, axis=1, keepdims=True) * scale

    total = total_of(recv1, pl.ds(ext_at, HEAD))
    far_scale = lax.rsqrt((stat[:, 64:65] + stat[:, 80:81]) / width + EPSILON)
    low8 = lax.broadcasted_iota(jnp.int32, (16, HEAD), 0) < 8
    places = jnp.where(
        low8, recv1[0, :, stat_at : stat_at + HEAD].astype(F32), recv1[mid, :, stat_at : stat_at + HEAD].astype(F32)
    )
    far_table = rope_tables(places[:, 96:97] * 256.0 + places[:, 112:113], inv_ref[...])
    far_query = rope(total * far_scale, far_table).astype(BF16)

    chunk = min(512, slots)
    n_chunk = slots // chunk
    contract = (((1,), (1,)), ((), ()))
    low_chunk = lax.broadcasted_iota(jnp.int32, (16, chunk), 0) < 8
    live = jnp.where(low_chunk, split_ref[0, 0], split_ref[0, 1])

    def scores_of(c, best):
        far_best, near_best = best
        at = pl.ds(pl.multiple_of(c * chunk, chunk), chunk)
        a = lax.dot_general(far_query, far[0, at, 0:HEAD], contract, preferred_element_type=F32)
        b = lax.dot_general(far_query, far[1, at, 0:HEAD], contract, preferred_element_type=F32)
        slot = lax.broadcasted_iota(jnp.int32, (16, chunk), 1) + c * chunk
        value = jnp.where(slot < live, jnp.where(low_chunk, a, b) * scale, NEG)
        s["fscore"][:, at] = value
        far_best = jnp.maximum(far_best, jnp.max(value, axis=1, keepdims=True))
        near = lax.dot_general(queries, pack[at, 0:HEAD], contract, preferred_element_type=F32)
        slot = lax.broadcasted_iota(jnp.int32, (HEADS * 16, chunk), 1) + c * chunk
        value = jnp.where((slot >= seg_start) & (slot < seg_end), near * scale, NEG)
        s["score"][:, at] = value
        return far_best, jnp.maximum(near_best, jnp.max(value, axis=1, keepdims=True))

    far_max, row_max = lax.fori_loop(0, n_chunk, scores_of, (jnp.full((16, 1), NEG, F32), own), unroll=True)
    own_weight = jnp.exp(own - row_max).astype(BF16).astype(F32)

    def sums_of(c, carry):
        far_totals, far_sum, totals, summed = carry
        at = pl.ds(pl.multiple_of(c * chunk, chunk), chunk)
        w = jnp.exp(s["fscore"][:, at] - far_max).astype(BF16)
        a = jnp.dot(w, far[0, at, HEAD:], preferred_element_type=F32)
        b = jnp.dot(w, far[1, at, HEAD:], preferred_element_type=F32)
        far_totals = far_totals + jnp.sum(w.astype(F32), axis=1, keepdims=True)
        far_sum = far_sum + jnp.where(low8, a, b)
        w = jnp.exp(s["score"][:, at] - row_max).astype(BF16)
        summed = summed + jnp.dot(w, pack[at, HEAD:], preferred_element_type=F32)
        return far_totals, far_sum, totals + jnp.sum(w.astype(F32), axis=1, keepdims=True), summed

    far_totals, far_sum, totals, summed = lax.fori_loop(
        0, n_chunk, sums_of,
        (jnp.zeros((16, 1), F32), jnp.zeros((16, HEAD), F32), own_weight, own_weight * values),
        unroll=True,
    )
    far_out = far_sum / far_totals
    far_lse = jnp.broadcast_to(far_max + jnp.log(far_totals), (16, HEAD))
    attended = summed / totals
    s["att"][...] = attended
    s["lse"][...] = jnp.broadcast_to(row_max + jnp.log(totals), (HEADS * 16, HEAD))
    mixed = s["mixed"]
    for h in range(HEADS):
        mixed[me, :, h * HEAD : (h + 1) * HEAD] = attended[h * 16 : (h + 1) * 16].astype(BF16)

    first_out = s["att"][pl.ds(0, HEADS, stride=16), :]
    first_lse = s["lse"][pl.ds(0, HEADS, stride=16), :]
    near_out = jnp.concatenate([first_out, first_out], axis=0)
    near_lse = jnp.concatenate([first_lse, first_lse], axis=0)
    owned = jnp.where(low8, 0, mid) == me
    peak = jnp.maximum(far_lse, near_lse)
    fa = jnp.exp(far_lse - peak)
    na = jnp.exp(near_lse - peak)
    part_out = jnp.where(owned, (fa * far_out + na * near_out) / (fa + na), far_out)
    part_lse = jnp.where(owned, peak + jnp.log(fa + na), far_lse)
    high = part_lse.astype(BF16).astype(F32)
    middle = (part_lse - high).astype(BF16).astype(F32)
    low = part_lse - high - middle
    mixed[me, :, qw : qw + HEAD] = part_out.astype(BF16)
    mixed[me, :, qw + HEAD :] = jnp.where(lane16 < 32, high, jnp.where(lane16 < 64, middle, low)).astype(BF16)
    spread_req("p2", lambda p: mixed.at[me], mixed)
    sent("p1", s["send1"], n_req - 1)
    load_wo.wait()
    arrived("p2", mixed, n_req - 1)

    parts = []
    for p in range(n_req):
        part = mixed[p, :, qw + HEAD :].astype(F32)
        parts.append(part[:, 0:1] + part[:, 32:33] + part[:, 64:65])
    peak = functools.reduce(jnp.maximum, parts)
    den = jnp.zeros((16, 1), F32)
    num = jnp.zeros((16, HEAD), F32)
    for p in range(n_req):
        w = jnp.exp(parts[p] - peak)
        den = den + w
        num = num + w * mixed[p, :, qw : qw + HEAD].astype(F32)
    long_out = num / den
    lhs = s["lhs"]
    lhs[...] = mixed[:, :, 0:qw]
    first = lax.broadcasted_iota(jnp.int32, (16, qw), 0) == 0
    for j in range(2):
        flat = jnp.concatenate([long_out[j * 8 + h : j * 8 + h + 1] for h in range(HEADS)], axis=1)
        block = mixed[j * mid, :, 0:qw].astype(F32)
        lhs[j * mid] = jnp.where(first, jnp.broadcast_to(flat, (16, qw)), block).astype(BF16)

    send3, recv3, res = s["send3"], s["recv3"], s["res"]
    for h in range(n_half):
        part = jnp.dot(lhs[...].reshape(rows, qw), s["wo"][:, pl.ds(h * hcols, hcols)], preferred_element_type=F32)
        send3[h] = part.astype(BF16).reshape(n_head, blk, hcols)
        spread_head("p3", lambda p, h=h: send3.at[h, p], recv3.at[h], h)
    sent("p2", mixed, n_req - 1)

    def block_total(buffer, mine, h):
        value = mine[h, mz].astype(F32)
        for k in range(1, n_head):
            value = value + buffer[h, lax.rem(mz + k, n_head)].astype(F32)
        return value

    for h in range(n_half):
        arrived("p3", recv3.at[h], n_head - 1, h)
        res[h, mz] = (xin[h, mz].astype(F32) + block_total(recv3, send3, h)).astype(BF16)
        spread_head("p4", lambda p, h=h: res.at[h, mz], res.at[h], h)
    for h in range(n_half):
        sent("p3", send3.at[h], n_head - 1, h)
    for h in range(n_half):
        arrived("p4", res.at[h], n_head - 1, h)

    squares = normed(res, gain2_ref)
    n_part = len(ff_parts)

    def along(side, k):
        if side == 0:
            c = lax.rem(mx + k, SIDE)
            return c, {"req": c * SIDE + my}
        c = lax.rem(my + k, SIDE)
        return c, {"req": mx * SIDE + c}

    coordinate = (mx, my)
    for g, (begin, end) in enumerate(ff_parts):
        buf = s[f"fs{g}"]

        @pl.loop(begin, end, unroll=True)
        def _(c, g=g, buf=buf, begin=begin):
            part = jnp.dot(
                s["xg"][...], s["wgu"][:, pl.ds(pl.multiple_of(c * 256, 256), 256)], preferred_element_type=F32
            ).astype(BF16).reshape(SIDE, SIDE, 16, 256)
            at = pl.ds(pl.multiple_of((c - begin) * 256, 256), 256)
            for a in range(SIDE):
                if g % 2 == 0:
                    buf[a, :, :, at] = part[a]
                else:
                    buf[a, :, :, at] = part[:, a]

        if g == 0:
            at = pl.ds((end - begin) * 256, HEAD)
            buf[:, :, :, at] = split_two(squares, lanes).reshape(SIDE, SIDE, 16, HEAD)
        for k in (2, 1, 3):
            c, peer = along(g % 2, k)
            remote(buf.at[c], s[f"fr{g}"].at[coordinate[g % 2]], "f1", g, peer).start()
    for h in range(n_half):
        sent("p4", res.at[h], n_head - 1, h)

    for g, (begin, end) in enumerate(ff_parts):
        side = g % 2
        buf, got, turn = s[f"fs{g}"], s[f"fr{g}"], s[f"ft{g}"]
        arrived("f1", got, SIDE - 1, g)
        mine = coordinate[side]

        @pl.loop(0, SIDE, unroll=True)
        def _(b, g=g, buf=buf, got=got, turn=turn, mine=mine, begin=begin, end=end):
            value = buf[mine, b].astype(F32)
            for k in range(1, SIDE):
                value = value + got[lax.rem(mine + k, SIDE), b].astype(F32)
            turn[b] = value.astype(BF16)
            if g == 0:
                stat = value[:, (end - begin) * 256 :]
                turn[b, :, pl.ds((end - begin) * 256, HEAD)] = split_two(stat[:, 0:1] + stat[:, 64:65], lane16)

        for k in (2, 1, 3):
            c, peer = along(1 - side, k)
            remote(turn.at[c], s[f"fu{g}"].at[coordinate[1 - side]], "f2", g, peer).start()

    ff_scale = None
    hid = [s[f"hid{w}"] for w in range(len(SETS))]
    for g, (begin, end) in enumerate(ff_parts):
        side = g % 2
        turn, got = s[f"ft{g}"], s[f"fu{g}"]
        arrived("f2", got, SIDE - 1, g)
        mine = coordinate[1 - side]

        def turned(at, turn=turn, got=got, mine=mine):
            value = turn[mine, :, at].astype(F32)
            for k in range(1, SIDE):
                value = value + got[lax.rem(mine + k, SIDE), :, at].astype(F32)
            return value

        if g == 0:
            stat = turned(pl.ds((end - begin) * 256, HEAD))
            ff_scale = lax.rsqrt((stat[:, 0:1] + stat[:, 64:65]) / width + EPSILON)
        which = next(w for w, members in enumerate(SETS) if g in members)
        base = ff_parts[SETS[which][0]][0]
        for c in range(begin, end):
            both = turned(pl.ds((c - begin) * 256, 256)) * ff_scale
            gate, up = both[:, :HEAD], both[:, HEAD:]
            hid[which][me, :, pl.ds((c - base) * HEAD, HEAD)] = (gate / (1.0 + jnp.exp(-gate)) * up).astype(BF16)
        if g == SETS[which][-1]:
            spread_req("p6", lambda p, which=which: hid[which].at[me], hid[which], which)
    for g in range(n_part):
        sent("f1", s[f"fs{g}"], SIDE - 1, g)
        sent("f2", s[f"ft{g}"], SIDE - 1, g)

    load_wd.wait()
    send7, recv7, oblk, out, down = s["send7"], s["recv7"], s["oblk"], s["out"], s["down"]
    done = 0
    for which, wide in enumerate(wides):
        arrived("p6", hid[which], n_req - 1, which)
        for h in range(n_half):
            at = pl.ds(h * hcols, hcols)
            part = jnp.dot(
                hid[which][...].reshape(rows, wide), s["wd"][pl.ds(done, wide), at], preferred_element_type=F32
            )
            if which > 0:
                part = down[:, at] + part
            if which < len(SETS) - 1:
                down[:, at] = part
            else:
                send7[h] = part.astype(BF16).reshape(n_head, blk, hcols)
                spread_head("p7", lambda p, h=h: send7.at[h, p], recv7.at[h], h)
        done += wide
    for which in range(len(SETS)):
        sent("p6", hid[which], n_req - 1, which)

    def hand_over(k, h):
        return remote(oblk.at[h], xin.at[h, mz], "in", h, {"section": 1, **head_peer(k)})

    for h in range(n_half):
        arrived("p7", recv7.at[h], n_head - 1, h)
        oblk[h] = (res[h, mz].astype(F32) + block_total(recv7, send7, h)).astype(BF16)

        @pl.when(sec == 0)
        def _(h=h):
            for k in ring + [0]:
                hand_over(k, h).start()

        @pl.when(sec == 1)
        def _(h=h):
            out[h, mz] = oblk[h]
            spread_head("p8", lambda p: oblk.at[h], out.at[h], h)

    for h in range(n_half):
        sent("p7", send7.at[h], n_head - 1, h)

    @pl.when(sec == 0)
    def _():
        remote(xin, out, "back", 0, {"section": 1}).wait_recv()
        for h in range(n_half):
            remote(xin.at[h], xin.at[h], "in", h, {"section": 1}).wait_send()

    @pl.when(sec == 1)
    def _():
        for h in range(n_half):
            arrived("p8", out.at[h], n_head - 1, h)

    for h in range(n_half):
        out_ref[:, :, pl.ds(h * hcols, hcols)] = out[h]

    @pl.when(sec == 1)
    def _():
        for h in range(n_half):
            sent("p8", out.at[h], n_head - 1, h)
        remote(xin, out, "back", 0, {"section": 0}).wait_send()


def local(
    tokens,
    attention_gain,
    query_key_value_weight,
    head_output_weight,
    feedforward_gain,
    gate_up,
    down_weight,
    packed_cache,
    long_cache,
    lengths,
    long_split,
):
    n_req = lax.axis_size("req")
    n_head = lax.axis_size("head")
    rows, cols = tokens.shape
    blk = rows // n_head
    qkv = query_key_value_weight.shape[3]
    qw = head_output_weight.shape[2]
    ff = down_weight.shape[1]
    slots = packed_cache.shape[1]
    assert slots == long_cache.shape[2] and rows == n_req * 16 and n_req == SIDE * SIDE
    half = (PIECES, n_head, blk, cols // PIECES)
    n = ff // HEAD
    cuts = [sum(PARTS[:g]) * n // sum(PARTS) for g in range(len(PARTS) + 1)]
    ff_parts = tuple(zip(cuts[:-1], cuts[1:]))
    wides = [(ff_parts[members[-1]][1] - ff_parts[members[0]][0]) * HEAD for members in SETS]
    freq_ids = np.arange(HEAD // 2, dtype=np.float32)
    inverse = np.float32(1.0) / np.power(np.float32(10000.0), freq_ids * np.float32(2.0) / np.float32(HEAD))
    inverse = jnp.asarray(np.concatenate([inverse, inverse])[None].astype(np.float32))
    vmem = pl.BlockSpec(memory_space=pltpu.VMEM)
    hbm = pl.BlockSpec(memory_space=pl.ANY)
    smem = pl.BlockSpec(memory_space=pltpu.SMEM)
    scratch = dict(
        wqkv=pltpu.VMEM((cols, qkv), BF16),
        wo=pltpu.VMEM((qw, cols), BF16),
        raw=pltpu.VMEM((cols, 2, ff), BF16),
        wgu=pltpu.VMEM((cols, 2 * ff), BF16),
        wd=pltpu.VMEM((ff, cols), BF16),
        pack=pltpu.VMEM((slots, 2 * HEAD), BF16),
        far=pltpu.VMEM((2, slots, 2 * HEAD), BF16),
        xin=pltpu.VMEM(half, BF16),
        xg=pltpu.VMEM((rows, cols), BF16),
        send1=pltpu.VMEM((n_req, 16, qkv + 2 * HEAD), BF16),
        recv1=pltpu.VMEM((n_req, 16, qkv + 2 * HEAD), BF16),
        ext=pltpu.VMEM((16, HEAD), F32),
        q=pltpu.VMEM((HEADS, 16, HEAD), BF16),
        score=pltpu.VMEM((HEADS * 16, slots), F32),
        fscore=pltpu.VMEM((16, slots), F32),
        att=pltpu.VMEM((HEADS * 16, HEAD), F32),
        lse=pltpu.VMEM((HEADS * 16, HEAD), F32),
        mixed=pltpu.VMEM((n_req, 16, qw + 2 * HEAD), BF16),
        lhs=pltpu.VMEM((n_req, 16, qw), BF16),
        send3=pltpu.VMEM(half, BF16),
        recv3=pltpu.VMEM(half, BF16),
        res=pltpu.VMEM(half, BF16),
        down=pltpu.VMEM((rows, cols), F32),
        send7=pltpu.VMEM(half, BF16),
        recv7=pltpu.VMEM(half, BF16),
        oblk=pltpu.VMEM((PIECES, blk, cols // PIECES), BF16),
        out=pltpu.VMEM(half, BF16),
        wsem=pltpu.SemaphoreType.DMA((6 + PIECES,)),
    )
    for w, wide in enumerate(wides):
        scratch[f"hid{w}"] = pltpu.VMEM((n_req, 16, wide), BF16)
    for g, (begin, end) in enumerate(ff_parts):
        wide = (end - begin) * 256 + (HEAD if g == 0 else 0)
        scratch[f"fs{g}"] = pltpu.VMEM((SIDE, SIDE, 16, wide), BF16)
        scratch[f"fr{g}"] = pltpu.VMEM((SIDE, SIDE, 16, wide), BF16)
        scratch[f"ft{g}"] = pltpu.VMEM((SIDE, 16, wide), BF16)
        scratch[f"fu{g}"] = pltpu.VMEM((SIDE, 16, wide), BF16)
    for name, count in dict(
        p1=1, p2=1, p3=PIECES, p4=PIECES, f1=len(PARTS), f2=len(PARTS), p6=len(SETS), p7=PIECES, p8=PIECES,
        **{"in": PIECES}, back=1,
    ).items():
        scratch["ss_" + name] = pltpu.SemaphoreType.DMA((count,))
        scratch["rs_" + name] = pltpu.SemaphoreType.DMA((count,))
    names = list(scratch)

    def body(*refs):
        plain, rest = refs[:13], refs[13:]
        kernel((n_req, n_head, cols * n_req), ff_parts, wides, *plain, dict(zip(names, rest)))

    out = pl.pallas_call(
        body,
        out_shape=jax.ShapeDtypeStruct((n_head, blk, cols), BF16),
        in_specs=[smem, hbm, vmem, hbm, hbm, vmem, hbm, hbm, hbm, hbm, vmem, vmem],
        out_specs=vmem,
        scratch_shapes=[scratch[name] for name in names],
        compiler_params=pltpu.CompilerParams(
            collective_id=0, has_side_effects=True, vmem_limit_bytes=56 * 2**20
        ),
        name="two_layers",
    )(
        long_split.T,
        tokens.reshape(n_head, blk, cols),
        attention_gain,
        query_key_value_weight.reshape(cols, qkv),
        head_output_weight.reshape(qw, cols),
        feedforward_gain,
        gate_up.reshape(cols, 2, ff),
        down_weight.reshape(ff, cols),
        packed_cache.reshape(slots, 2 * HEAD),
        long_cache.reshape(2, slots, 2 * HEAD),
        lengths,
        inverse,
    )
    return out.reshape(1, rows, cols)


def solution(mesh):
    placed = (
        P(None, "req"),
        P("section", "req"),
        P("section", "req", "head", None),
        P("section", "head", None, "req"),
        P("section", "req"),
        P("section", "req", None, "head"),
        P("section", "head", "req"),
        P("section", "req", "head", None),
        P("section", None, "req", "head", None),
        P("req", None),
        P(None, "req"),
    )
    return jax.shard_map(
        local, mesh=mesh, in_specs=placed, out_specs=P("section", None, "req"), check_vma=False
    )
```

```python
import functools
import math

import jax
import jax.numpy as jnp
import numpy as np
from jax import lax
from jax.experimental import pallas as pl
from jax.experimental.pallas import tpu as pltpu
from jax.sharding import PartitionSpec as P

HEAD = 128
HEADS = 8
LONG = 16384
EPSILON = 1e-05
NEG = -1e30
F32 = jnp.float32
BF16 = jnp.bfloat16
MESH = pl.DeviceIdType.MESH
SIDE = 4
FAR_FIRST = sorted(
    ((a, b) for a in range(SIDE) for b in range(SIDE) if a or b),
    key=lambda d: (-(d[0] > 0) - (d[1] > 0), -min(d[0], SIDE - d[0]) - min(d[1], SIDE - d[1]), d),
)


PIECES = 2
PARTS = (1, 1, 2, 2, 2, 2, 2, 2)
SETS = ((0, 1), (2, 3), (4, 5), (6, 7))


def split_two(value, lanes):
    high = value.astype(BF16).astype(F32)
    return jnp.where(lanes < 64, high, value - high).astype(BF16)


def rope(block, table):
    swapped = jnp.concatenate([block[:, HEAD // 2 :], block[:, : HEAD // 2]], axis=1)
    return block * table[0] + swapped * table[1]


def rope_tables(position, inverse):
    angles = position * inverse
    lane = lax.broadcasted_iota(jnp.int32, angles.shape, 1)
    sine = jnp.sin(angles)
    return jnp.cos(angles), jnp.where(lane < HEAD // 2, -sine, sine)


def kernel(dims, ff_parts, wides, split_ref, tok_hbm, gain1_ref, wqkv_hbm, wo_hbm, gain2_ref, raw_hbm, wd_hbm, pack_hbm, far_hbm,
           len_ref, inv_ref, out_ref, scratch):
    n_req, n_head, width = dims
    s = scratch
    sec = lax.axis_index("section")
    me = lax.axis_index("req")
    mz = lax.axis_index("head")
    mx, my = lax.div(me, SIDE), lax.rem(me, SIDE)
    xin = s["xin"]
    n_half, _, blk, hcols = xin.shape
    cols = n_half * hcols
    rows = n_head * blk
    slots = s["pack"].shape[0]
    qw = HEADS * HEAD
    ff = s["wd"].shape[0]
    scale = 1.0 / math.sqrt(HEAD)
    mid = n_req // 2
    ext_at = qw + 2 * HEAD
    stat_at = ext_at + HEAD

    def remote(source, target, name, where, peer):
        return pltpu.make_async_remote_copy(
            src_ref=source, dst_ref=target, send_sem=s["ss_" + name].at[where], recv_sem=s["rs_" + name].at[where],
            device_id=peer, device_id_type=MESH,
        )

    def req_peer(step):
        return {"req": lax.rem(mx + step[0], SIDE) * SIDE + lax.rem(my + step[1], SIDE)}

    ring = sorted(range(1, n_head), key=lambda k: (-min(k, n_head - k), k))

    def head_peer(k):
        return {"head": lax.rem(mz + k, n_head)}

    def spread_req(name, source, target, where=0):
        for step in FAR_FIRST:
            peer = req_peer(step)
            remote(source(peer["req"]), target.at[me], name, where, peer).start()

    def spread_head(name, source, target, where=0):
        for k in ring:
            peer = head_peer(k)
            remote(source(peer["head"]), target.at[mz], name, where, peer).start()

    def arrived(name, target, count, where=0):
        whole = target.at[pl.ds(0, count)]
        remote(whole, whole, name, where, {"section": 1 - sec}).wait_recv()

    def sent(name, source, count, where=0):
        whole = source.at[pl.ds(0, count)]
        remote(whole, whole, name, where, {"section": 1 - sec}).wait_send()

    def load(source, target, n):
        return pltpu.make_async_copy(source, target, s["wsem"].at[n])

    load_qkv = load(wqkv_hbm, s["wqkv"], 0)
    load_raw = load(raw_hbm, s["raw"], 1)
    load_pack = load(pack_hbm, s["pack"], 2)
    load_far = load(far_hbm, s["far"], 3)
    load_wo = load(wo_hbm, s["wo"], 4)
    load_wd = load(wd_hbm, s["wd"], 5)
    load_qkv.start()

    @pl.when(sec == 0)
    def _():
        for h in range(n_half):
            load(tok_hbm.at[:, :, pl.ds(h * hcols, hcols)], xin.at[h], 6 + h).start()

    barrier = pltpu.get_barrier_semaphore()

    def greet_section():
        for k in ring + [0]:
            pl.semaphore_signal(barrier, inc=1, device_id={"section": 1 - sec, **head_peer(k)}, device_id_type=MESH)

    pl.when(sec == 1)(greet_section)
    for step in FAR_FIRST:
        pl.semaphore_signal(barrier, inc=1, device_id=req_peer(step), device_id_type=MESH)
    for k in ring:
        pl.semaphore_signal(barrier, inc=1, device_id=head_peer(k), device_id_type=MESH)
    pl.when(sec == 0)(greet_section)

    for other in (load_raw, load_pack, load_far, load_wo, load_wd):
        other.start()

    def lane_sum(mask, shape):
        lens = jnp.broadcast_to(len_ref[...].astype(F32), shape)
        return jnp.sum(jnp.where(mask, lens, 0.0), axis=1, keepdims=True)

    r16 = lax.broadcasted_iota(jnp.int32, (16, 16), 0)
    k16 = lax.broadcasted_iota(jnp.int32, (16, 16), 1)
    is_long = (lax.broadcasted_iota(jnp.int32, (16, 1), 0) == 0) & ((me == 0) | (me == mid))
    position = lane_sum(k16 == r16, (16, 16)) + jnp.where(is_long, float(LONG), 0.0)

    lanes = lax.broadcasted_iota(jnp.int32, (rows, HEAD), 1)
    lane16 = lax.broadcasted_iota(jnp.int32, (16, HEAD), 1)

    def normed(source, gain_ref):
        squares = jnp.zeros((rows, 1), F32)
        for h in range(n_half):
            at = pl.ds(h * hcols, hcols)
            x = source[h].reshape(rows, hcols).astype(F32)
            squares = squares + jnp.sum(x * x, axis=1, keepdims=True)
            s["xg"][:, at] = (x * gain_ref[:, at].astype(F32)).astype(BF16)
        return squares

    def first_products():
        squares = normed(xin, gain1_ref)
        load_qkv.wait()

        @pl.loop(0, ext_at // 256, unroll=True)
        def _(c):
            at = pl.ds(pl.multiple_of(c * 256, 256), 256)
            part = jnp.dot(s["xg"][...], s["wqkv"][:, at], preferred_element_type=F32)
            s["send1"][:, :, at] = part.astype(BF16).reshape(n_req, 16, 256)

        ext = s["ext"]
        for j in range(2):
            row = s["send1"][j * mid, :, 0:qw].astype(F32)[0:1]
            for h in range(HEADS):
                ext[j * 8 + h : j * 8 + h + 1, :] = row[:, h * HEAD : (h + 1) * HEAD]
        head = ext[...].astype(BF16)
        first = position[0:1]
        upper = jnp.floor(first * (1.0 / 256.0))
        lower = first - 256.0 * upper
        row16 = lax.broadcasted_iota(jnp.int32, (16, HEAD), 0)
        far_squares = jnp.where(row16 < 8, squares[0:1], squares[mid * 16 : mid * 16 + 1])
        far_high = far_squares.astype(BF16).astype(F32)
        common = jnp.where(
            lane16 < 80, far_high, jnp.where(lane16 < 96, far_squares - far_high, jnp.where(lane16 < 112, upper, lower))
        )
        high = squares.astype(BF16).astype(F32)
        pair = jnp.where(lanes < 32, high, squares - high).reshape(n_req, 16, HEAD)
        for g in range(n_req):
            s["send1"][g, :, ext_at : ext_at + HEAD] = head
            s["send1"][g, :, stat_at : stat_at + HEAD] = jnp.where(lane16 < 64, pair[g], common).astype(BF16)

    def split_gate():
        load_raw.wait()
        raw, wgu = s["raw"], s["wgu"]

        @pl.loop(0, cols // 16)
        def _(k):
            at = pl.ds(pl.multiple_of(k * 16, 16), 16)
            for c in range(ff // HEAD):
                source = pl.ds(c * HEAD, HEAD)
                wgu[at, pl.ds(c * 256, HEAD)] = raw[at, 0, source]
                wgu[at, pl.ds(c * 256 + HEAD, HEAD)] = raw[at, 1, source]

    @pl.when(sec == 0)
    def _():
        for h in range(n_half):
            load(tok_hbm.at[:, :, pl.ds(h * hcols, hcols)], xin.at[h], 6 + h).wait()
        first_products()

    pl.semaphore_wait(barrier, n_req - 1 + n_head - 1 + n_head)

    @pl.when(sec == 1)
    def _():
        split_gate()
        for h in range(n_half):
            remote(xin.at[h], xin.at[h], "in", h, {"section": 0}).wait_recv()
        remote(xin, s["out"], "back", 0, {"section": 0}).start()
        first_products()

    spread_req("p1", lambda p: s["send1"].at[p], s["recv1"])
    s["recv1"][me] = s["send1"][me]

    @pl.when(sec == 0)
    def _():
        split_gate()

    own_table = rope_tables(position, inv_ref[...])
    r_id = lax.broadcasted_iota(jnp.int32, (16 * HEADS, 16), 0) & 15
    k_id = lax.broadcasted_iota(jnp.int32, (16 * HEADS, 16), 1)
    seg_end = lane_sum(k_id <= r_id, (16 * HEADS, 16)).astype(jnp.int32)
    seg_start = lane_sum(k_id < r_id, (16 * HEADS, 16)).astype(jnp.int32)
    load_pack.wait()
    load_far.wait()
    pack, far = s["pack"], s["far"]
    recv1 = s["recv1"]
    arrived("p1", recv1, n_req - 1)

    def total_of(ref, at):
        value = ref[0, :, at].astype(F32)
        for p in range(1, ref.shape[0]):
            value = value + ref[p, :, at].astype(F32)
        return value

    stat = total_of(recv1, pl.ds(stat_at, HEAD))
    row_scale = lax.rsqrt((stat[:, 0:1] + stat[:, 32:33]) / width + EPSILON)

    for h in range(HEADS):
        at = pl.ds(h * HEAD, HEAD)
        s["q"][h] = rope(total_of(recv1, at) * row_scale, own_table).astype(BF16)

    new_key = rope(total_of(recv1, pl.ds(qw, HEAD)) * row_scale, own_table).astype(BF16)
    new_value = (total_of(recv1, pl.ds(qw + HEAD, HEAD)) * row_scale).astype(BF16)
    queries = s["q"][...].reshape(HEADS * 16, HEAD)
    keys = jnp.concatenate([new_key.astype(F32)] * HEADS, axis=0)
    values = jnp.concatenate([new_value.astype(F32)] * HEADS, axis=0)
    own = jnp.sum(queries.astype(F32) * keys, axis=1, keepdims=True) * scale

    total = total_of(recv1, pl.ds(ext_at, HEAD))
    far_scale = lax.rsqrt((stat[:, 64:65] + stat[:, 80:81]) / width + EPSILON)
    low8 = lax.broadcasted_iota(jnp.int32, (16, HEAD), 0) < 8
    places = jnp.where(
        low8, recv1[0, :, stat_at : stat_at + HEAD].astype(F32), recv1[mid, :, stat_at : stat_at + HEAD].astype(F32)
    )
    far_table = rope_tables(places[:, 96:97] * 256.0 + places[:, 112:113], inv_ref[...])
    far_query = rope(total * far_scale, far_table).astype(BF16)

    chunk = min(512, slots)
    n_chunk = slots // chunk
    contract = (((1,), (1,)), ((), ()))
    low_chunk = lax.broadcasted_iota(jnp.int32, (16, chunk), 0) < 8
    live = jnp.where(low_chunk, split_ref[0, 0], split_ref[0, 1])

    def scores_of(c, best):
        far_best, near_best = best
        at = pl.ds(pl.multiple_of(c * chunk, chunk), chunk)
        a = lax.dot_general(far_query, far[0, at, 0:HEAD], contract, preferred_element_type=F32)
        b = lax.dot_general(far_query, far[1, at, 0:HEAD], contract, preferred_element_type=F32)
        slot = lax.broadcasted_iota(jnp.int32, (16, chunk), 1) + c * chunk
        value = jnp.where(slot < live, jnp.where(low_chunk, a, b) * scale, NEG)
        s["fscore"][:, at] = value
        far_best = jnp.maximum(far_best, jnp.max(value, axis=1, keepdims=True))
        near = lax.dot_general(queries, pack[at, 0:HEAD], contract, preferred_element_type=F32)
        slot = lax.broadcasted_iota(jnp.int32, (HEADS * 16, chunk), 1) + c * chunk
        value = jnp.where((slot >= seg_start) & (slot < seg_end), near * scale, NEG)
        s["score"][:, at] = value
        return far_best, jnp.maximum(near_best, jnp.max(value, axis=1, keepdims=True))

    far_max, row_max = lax.fori_loop(0, n_chunk, scores_of, (jnp.full((16, 1), NEG, F32), own), unroll=True)
    own_weight = jnp.exp(own - row_max).astype(BF16).astype(F32)

    def sums_of(c, carry):
        far_totals, far_sum, totals, summed = carry
        at = pl.ds(pl.multiple_of(c * chunk, chunk), chunk)
        w = jnp.exp(s["fscore"][:, at] - far_max).astype(BF16)
        a = jnp.dot(w, far[0, at, HEAD:], preferred_element_type=F32)
        b = jnp.dot(w, far[1, at, HEAD:], preferred_element_type=F32)
        far_totals = far_totals + jnp.sum(w.astype(F32), axis=1, keepdims=True)
        far_sum = far_sum + jnp.where(low8, a, b)
        w = jnp.exp(s["score"][:, at] - row_max).astype(BF16)
        summed = summed + jnp.dot(w, pack[at, HEAD:], preferred_element_type=F32)
        return far_totals, far_sum, totals + jnp.sum(w.astype(F32), axis=1, keepdims=True), summed

    far_totals, far_sum, totals, summed = lax.fori_loop(
        0, n_chunk, sums_of,
        (jnp.zeros((16, 1), F32), jnp.zeros((16, HEAD), F32), own_weight, own_weight * values),
        unroll=True,
    )
    far_out = far_sum / far_totals
    far_lse = jnp.broadcast_to(far_max + jnp.log(far_totals), (16, HEAD))
    attended = summed / totals
    s["att"][...] = attended
    s["lse"][...] = jnp.broadcast_to(row_max + jnp.log(totals), (HEADS * 16, HEAD))
    mixed = s["mixed"]
    for h in range(HEADS):
        mixed[me, :, h * HEAD : (h + 1) * HEAD] = attended[h * 16 : (h + 1) * 16].astype(BF16)

    first_out = s["att"][pl.ds(0, HEADS, stride=16), :]
    first_lse = s["lse"][pl.ds(0, HEADS, stride=16), :]
    near_out = jnp.concatenate([first_out, first_out], axis=0)
    near_lse = jnp.concatenate([first_lse, first_lse], axis=0)
    owned = jnp.where(low8, 0, mid) == me
    peak = jnp.maximum(far_lse, near_lse)
    fa = jnp.exp(far_lse - peak)
    na = jnp.exp(near_lse - peak)
    part_out = jnp.where(owned, (fa * far_out + na * near_out) / (fa + na), far_out)
    part_lse = jnp.where(owned, peak + jnp.log(fa + na), far_lse)
    high = part_lse.astype(BF16).astype(F32)
    middle = (part_lse - high).astype(BF16).astype(F32)
    low = part_lse - high - middle
    mixed[me, :, qw : qw + HEAD] = part_out.astype(BF16)
    mixed[me, :, qw + HEAD :] = jnp.where(lane16 < 32, high, jnp.where(lane16 < 64, middle, low)).astype(BF16)
    spread_req("p2", lambda p: mixed.at[me], mixed)
    sent("p1", s["send1"], n_req - 1)
    load_wo.wait()
    arrived("p2", mixed, n_req - 1)

    parts = []
    for p in range(n_req):
        part = mixed[p, :, qw + HEAD :].astype(F32)
        parts.append(part[:, 0:1] + part[:, 32:33] + part[:, 64:65])
    peak = functools.reduce(jnp.maximum, parts)
    den = jnp.zeros((16, 1), F32)
    num = jnp.zeros((16, HEAD), F32)
    for p in range(n_req):
        w = jnp.exp(parts[p] - peak)
        den = den + w
        num = num + w * mixed[p, :, qw : qw + HEAD].astype(F32)
    long_out = num / den
    lhs = s["lhs"]
    lhs[...] = mixed[:, :, 0:qw]
    first = lax.broadcasted_iota(jnp.int32, (16, qw), 0) == 0
    for j in range(2):
        flat = jnp.concatenate([long_out[j * 8 + h : j * 8 + h + 1] for h in range(HEADS)], axis=1)
        block = mixed[j * mid, :, 0:qw].astype(F32)
        lhs[j * mid] = jnp.where(first, jnp.broadcast_to(flat, (16, qw)), block).astype(BF16)

    send3, recv3, res = s["send3"], s["recv3"], s["res"]
    for h in range(n_half):
        part = jnp.dot(lhs[...].reshape(rows, qw), s["wo"][:, pl.ds(h * hcols, hcols)], preferred_element_type=F32)
        send3[h] = part.astype(BF16).reshape(n_head, blk, hcols)
        spread_head("p3", lambda p, h=h: send3.at[h, p], recv3.at[h], h)
    sent("p2", mixed, n_req - 1)

    def block_total(buffer, mine, h):
        value = mine[h, mz].astype(F32)
        for k in range(1, n_head):
            value = value + buffer[h, lax.rem(mz + k, n_head)].astype(F32)
        return value

    for h in range(n_half):
        arrived("p3", recv3.at[h], n_head - 1, h)
        res[h, mz] = (xin[h, mz].astype(F32) + block_total(recv3, send3, h)).astype(BF16)
        spread_head("p4", lambda p, h=h: res.at[h, mz], res.at[h], h)
    for h in range(n_half):
        sent("p3", send3.at[h], n_head - 1, h)
    for h in range(n_half):
        arrived("p4", res.at[h], n_head - 1, h)

    squares = normed(res, gain2_ref)
    n_part = len(ff_parts)

    def along(side, k):
        if side == 0:
            c = lax.rem(mx + k, SIDE)
            return c, {"req": c * SIDE + my}
        c = lax.rem(my + k, SIDE)
        return c, {"req": mx * SIDE + c}

    coordinate = (mx, my)
    for g, (begin, end) in enumerate(ff_parts):
        buf = s[f"fs{g}"]

        @pl.loop(begin, end, unroll=True)
        def _(c, g=g, buf=buf, begin=begin):
            part = jnp.dot(
                s["xg"][...], s["wgu"][:, pl.ds(pl.multiple_of(c * 256, 256), 256)], preferred_element_type=F32
            ).astype(BF16).reshape(SIDE, SIDE, 16, 256)
            at = pl.ds(pl.multiple_of((c - begin) * 256, 256), 256)
            for a in range(SIDE):
                if g % 2 == 0:
                    buf[a, :, :, at] = part[a]
                else:
                    buf[a, :, :, at] = part[:, a]

        if g == 0:
            at = pl.ds((end - begin) * 256, HEAD)
            buf[:, :, :, at] = split_two(squares, lanes).reshape(SIDE, SIDE, 16, HEAD)
        for k in (2, 1, 3):
            c, peer = along(g % 2, k)
            remote(buf.at[c], s[f"fr{g}"].at[coordinate[g % 2]], "f1", g, peer).start()
    for h in range(n_half):
        sent("p4", res.at[h], n_head - 1, h)

    for g, (begin, end) in enumerate(ff_parts):
        side = g % 2
        buf, got, turn = s[f"fs{g}"], s[f"fr{g}"], s[f"ft{g}"]
        arrived("f1", got, SIDE - 1, g)
        mine = coordinate[side]

        @pl.loop(0, SIDE, unroll=True)
        def _(b, g=g, buf=buf, got=got, turn=turn, mine=mine, begin=begin, end=end):
            value = buf[mine, b].astype(F32)
            for k in range(1, SIDE):
                value = value + got[lax.rem(mine + k, SIDE), b].astype(F32)
            turn[b] = value.astype(BF16)
            if g == 0:
                stat = value[:, (end - begin) * 256 :]
                turn[b, :, pl.ds((end - begin) * 256, HEAD)] = split_two(stat[:, 0:1] + stat[:, 64:65], lane16)

        for k in (2, 1, 3):
            c, peer = along(1 - side, k)
            remote(turn.at[c], s[f"fu{g}"].at[coordinate[1 - side]], "f2", g, peer).start()

    ff_scale = None
    hid = [s[f"hid{w}"] for w in range(len(SETS))]
    for g, (begin, end) in enumerate(ff_parts):
        side = g % 2
        turn, got = s[f"ft{g}"], s[f"fu{g}"]
        arrived("f2", got, SIDE - 1, g)
        mine = coordinate[1 - side]

        def turned(at, turn=turn, got=got, mine=mine):
            value = turn[mine, :, at].astype(F32)
            for k in range(1, SIDE):
                value = value + got[lax.rem(mine + k, SIDE), :, at].astype(F32)
            return value

        if g == 0:
            stat = turned(pl.ds((end - begin) * 256, HEAD))
            ff_scale = lax.rsqrt((stat[:, 0:1] + stat[:, 64:65]) / width + EPSILON)
        which = next(w for w, members in enumerate(SETS) if g in members)
        base = ff_parts[SETS[which][0]][0]
        for c in range(begin, end):
            both = turned(pl.ds((c - begin) * 256, 256)) * ff_scale
            gate, up = both[:, :HEAD], both[:, HEAD:]
            hid[which][me, :, pl.ds((c - base) * HEAD, HEAD)] = (gate / (1.0 + jnp.exp(-gate)) * up).astype(BF16)
        if g == SETS[which][-1]:
            spread_req("p6", lambda p, which=which: hid[which].at[me], hid[which], which)
    for g in range(n_part):
        sent("f1", s[f"fs{g}"], SIDE - 1, g)
        sent("f2", s[f"ft{g}"], SIDE - 1, g)

    load_wd.wait()
    send7, recv7, oblk, out, down = s["send7"], s["recv7"], s["oblk"], s["out"], s["down"]
    done = 0
    for which, wide in enumerate(wides):
        arrived("p6", hid[which], n_req - 1, which)
        for h in range(n_half):
            at = pl.ds(h * hcols, hcols)
            part = jnp.dot(
                hid[which][...].reshape(rows, wide), s["wd"][pl.ds(done, wide), at], preferred_element_type=F32
            )
            if which > 0:
                part = down[:, at] + part
            if which < len(SETS) - 1:
                down[:, at] = part
            else:
                send7[h] = part.astype(BF16).reshape(n_head, blk, hcols)
                spread_head("p7", lambda p, h=h: send7.at[h, p], recv7.at[h], h)
        done += wide
    for which in range(len(SETS)):
        sent("p6", hid[which], n_req - 1, which)

    def hand_over(k, h):
        return remote(oblk.at[h], xin.at[h, mz], "in", h, {"section": 1, **head_peer(k)})

    for h in range(n_half):
        arrived("p7", recv7.at[h], n_head - 1, h)
        oblk[h] = (res[h, mz].astype(F32) + block_total(recv7, send7, h)).astype(BF16)

        @pl.when(sec == 0)
        def _(h=h):
            for k in ring + [0]:
                hand_over(k, h).start()

        @pl.when(sec == 1)
        def _(h=h):
            out[h, mz] = oblk[h]
            spread_head("p8", lambda p: oblk.at[h], out.at[h], h)

    for h in range(n_half):
        sent("p7", send7.at[h], n_head - 1, h)

    @pl.when(sec == 0)
    def _():
        remote(xin, out, "back", 0, {"section": 1}).wait_recv()
        for h in range(n_half):
            remote(xin.at[h], xin.at[h], "in", h, {"section": 1}).wait_send()

    @pl.when(sec == 1)
    def _():
        for h in range(n_half):
            arrived("p8", out.at[h], n_head - 1, h)

    for h in range(n_half):
        out_ref[:, :, pl.ds(h * hcols, hcols)] = out[h]

    @pl.when(sec == 1)
    def _():
        for h in range(n_half):
            sent("p8", out.at[h], n_head - 1, h)
        remote(xin, out, "back", 0, {"section": 0}).wait_send()


def local(
    tokens,
    attention_gain,
    query_key_value_weight,
    head_output_weight,
    feedforward_gain,
    gate_up,
    down_weight,
    packed_cache,
    long_cache,
    lengths,
    long_split,
):
    n_req = lax.axis_size("req")
    n_head = lax.axis_size("head")
    rows, cols = tokens.shape
    blk = rows // n_head
    qkv = query_key_value_weight.shape[3]
    qw = head_output_weight.shape[2]
    ff = down_weight.shape[1]
    slots = packed_cache.shape[1]
    assert slots == long_cache.shape[2] and rows == n_req * 16 and n_req == SIDE * SIDE
    half = (PIECES, n_head, blk, cols // PIECES)
    n = ff // HEAD
    cuts = [sum(PARTS[:g]) * n // sum(PARTS) for g in range(len(PARTS) + 1)]
    ff_parts = tuple(zip(cuts[:-1], cuts[1:]))
    wides = [(ff_parts[members[-1]][1] - ff_parts[members[0]][0]) * HEAD for members in SETS]
    freq_ids = np.arange(HEAD // 2, dtype=np.float32)
    inverse = np.float32(1.0) / np.power(np.float32(10000.0), freq_ids * np.float32(2.0) / np.float32(HEAD))
    inverse = jnp.asarray(np.concatenate([inverse, inverse])[None].astype(np.float32))
    vmem = pl.BlockSpec(memory_space=pltpu.VMEM)
    hbm = pl.BlockSpec(memory_space=pl.ANY)
    smem = pl.BlockSpec(memory_space=pltpu.SMEM)
    scratch = dict(
        wqkv=pltpu.VMEM((cols, qkv), BF16),
        wo=pltpu.VMEM((qw, cols), BF16),
        raw=pltpu.VMEM((cols, 2, ff), BF16),
        wgu=pltpu.VMEM((cols, 2 * ff), BF16),
        wd=pltpu.VMEM((ff, cols), BF16),
        pack=pltpu.VMEM((slots, 2 * HEAD), BF16),
        far=pltpu.VMEM((2, slots, 2 * HEAD), BF16),
        xin=pltpu.VMEM(half, BF16),
        xg=pltpu.VMEM((rows, cols), BF16),
        send1=pltpu.VMEM((n_req, 16, qkv + 2 * HEAD), BF16),
        recv1=pltpu.VMEM((n_req, 16, qkv + 2 * HEAD), BF16),
        ext=pltpu.VMEM((16, HEAD), F32),
        q=pltpu.VMEM((HEADS, 16, HEAD), BF16),
        score=pltpu.VMEM((HEADS * 16, slots), F32),
        fscore=pltpu.VMEM((16, slots), F32),
        att=pltpu.VMEM((HEADS * 16, HEAD), F32),
        lse=pltpu.VMEM((HEADS * 16, HEAD), F32),
        mixed=pltpu.VMEM((n_req, 16, qw + 2 * HEAD), BF16),
        lhs=pltpu.VMEM((n_req, 16, qw), BF16),
        send3=pltpu.VMEM(half, BF16),
        recv3=pltpu.VMEM(half, BF16),
        res=pltpu.VMEM(half, BF16),
        down=pltpu.VMEM((rows, cols), F32),
        send7=pltpu.VMEM(half, BF16),
        recv7=pltpu.VMEM(half, BF16),
        oblk=pltpu.VMEM((PIECES, blk, cols // PIECES), BF16),
        out=pltpu.VMEM(half, BF16),
        wsem=pltpu.SemaphoreType.DMA((6 + PIECES,)),
    )
    for w, wide in enumerate(wides):
        scratch[f"hid{w}"] = pltpu.VMEM((n_req, 16, wide), BF16)
    for g, (begin, end) in enumerate(ff_parts):
        wide = (end - begin) * 256 + (HEAD if g == 0 else 0)
        scratch[f"fs{g}"] = pltpu.VMEM((SIDE, SIDE, 16, wide), BF16)
        scratch[f"fr{g}"] = pltpu.VMEM((SIDE, SIDE, 16, wide), BF16)
        scratch[f"ft{g}"] = pltpu.VMEM((SIDE, 16, wide), BF16)
        scratch[f"fu{g}"] = pltpu.VMEM((SIDE, 16, wide), BF16)
    for name, count in dict(
        p1=1, p2=1, p3=PIECES, p4=PIECES, f1=len(PARTS), f2=len(PARTS), p6=len(SETS), p7=PIECES, p8=PIECES,
        **{"in": PIECES}, back=1,
    ).items():
        scratch["ss_" + name] = pltpu.SemaphoreType.DMA((count,))
        scratch["rs_" + name] = pltpu.SemaphoreType.DMA((count,))
    names = list(scratch)

    def body(*refs):
        plain, rest = refs[:13], refs[13:]
        kernel((n_req, n_head, cols * n_req), ff_parts, wides, *plain, dict(zip(names, rest)))

    out = pl.pallas_call(
        body,
        out_shape=pltpu.VMEM((n_head, blk, cols), BF16),
        in_specs=[smem, hbm, vmem, hbm, hbm, vmem, hbm, hbm, hbm, hbm, vmem, vmem],
        out_specs=vmem,
        scratch_shapes=[scratch[name] for name in names],
        compiler_params=pltpu.CompilerParams(
            collective_id=0, has_side_effects=True, vmem_limit_bytes=56 * 2**20
        ),
        name="two_layers",
    )(
        long_split.T,
        tokens.reshape(n_head, blk, cols),
        attention_gain,
        query_key_value_weight.reshape(cols, qkv),
        head_output_weight.reshape(qw, cols),
        feedforward_gain,
        gate_up.reshape(cols, 2, ff),
        down_weight.reshape(ff, cols),
        packed_cache.reshape(slots, 2 * HEAD),
        long_cache.reshape(2, slots, 2 * HEAD),
        lengths,
        inverse,
    )
    return out.reshape(1, rows, cols)


def solution(mesh):
    placed = (
        P(None, "req"),
        P("section", "req"),
        P("section", "req", "head", None),
        P("section", "head", None, "req"),
        P("section", "req"),
        P("section", "req", None, "head"),
        P("section", "head", "req"),
        P("section", "req", "head", None),
        P("section", None, "req", "head", None),
        P("req", None),
        P(None, "req"),
    )
    return jax.shard_map(
        local, mesh=mesh, in_specs=placed, out_specs=P("section", None, "req"), check_vma=False
    )
```

```python
import functools
import math

import jax
import jax.numpy as jnp
import numpy as np
from jax import lax
from jax.experimental import pallas as pl
from jax.experimental.pallas import tpu as pltpu
from jax.sharding import PartitionSpec as P

HEAD = 128
HEADS = 8
LONG = 16384
EPSILON = 1e-05
NEG = -1e30
F32 = jnp.float32
BF16 = jnp.bfloat16
MESH = pl.DeviceIdType.MESH
SIDE = 4
FAR_FIRST = sorted(
    ((a, b) for a in range(SIDE) for b in range(SIDE) if a or b),
    key=lambda d: (-(d[0] > 0) - (d[1] > 0), -min(d[0], SIDE - d[0]) - min(d[1], SIDE - d[1]), d),
)


PIECES = 2
PARTS = (1, 1, 2, 2, 2, 2, 2, 2)
SETS = ((0, 1), (2, 3), (4, 5), (6, 7))


def split_two(value, lanes):
    high = value.astype(BF16).astype(F32)
    return jnp.where(lanes < 64, high, value - high).astype(BF16)


def rope(block, table):
    swapped = jnp.concatenate([block[:, HEAD // 2 :], block[:, : HEAD // 2]], axis=1)
    return block * table[0] + swapped * table[1]


def rope_tables(position, inverse):
    angles = position * inverse
    lane = lax.broadcasted_iota(jnp.int32, angles.shape, 1)
    sine = jnp.sin(angles)
    return jnp.cos(angles), jnp.where(lane < HEAD // 2, -sine, sine)


def kernel(dims, ff_parts, wides, split_ref, tok_hbm, gain1_ref, wqkv_hbm, wo_hbm, gain2_ref, raw_hbm, wd_hbm, pack_hbm, far_hbm,
           len_ref, inv_ref, out_ref, scratch):
    n_req, n_head, width = dims
    s = scratch
    sec = lax.axis_index("section")
    me = lax.axis_index("req")
    mz = lax.axis_index("head")
    mx, my = lax.div(me, SIDE), lax.rem(me, SIDE)
    xin = s["xin"]
    n_half, _, blk, hcols = xin.shape
    cols = n_half * hcols
    rows = n_head * blk
    slots = s["pack"].shape[0]
    qw = HEADS * HEAD
    ff = s["wd"].shape[0]
    scale = 1.0 / math.sqrt(HEAD)
    mid = n_req // 2
    ext_at = qw + 2 * HEAD
    stat_at = ext_at + HEAD

    def remote(source, target, name, where, peer):
        return pltpu.make_async_remote_copy(
            src_ref=source, dst_ref=target, send_sem=s["ss_" + name].at[where], recv_sem=s["rs_" + name].at[where],
            device_id=peer, device_id_type=MESH,
        )

    def req_peer(step):
        return {"req": lax.rem(mx + step[0], SIDE) * SIDE + lax.rem(my + step[1], SIDE)}

    ring = sorted(range(1, n_head), key=lambda k: (-min(k, n_head - k), k))

    def head_peer(k):
        return {"head": lax.rem(mz + k, n_head)}

    def spread_req(name, source, target, where=0):
        for step in FAR_FIRST:
            peer = req_peer(step)
            remote(source(peer["req"]), target.at[me], name, where, peer).start()

    def spread_head(name, source, target, where=0):
        for k in ring:
            peer = head_peer(k)
            remote(source(peer["head"]), target.at[mz], name, where, peer).start()

    def arrived(name, target, count, where=0):
        whole = target.at[pl.ds(0, count)]
        remote(whole, whole, name, where, {"section": 1 - sec}).wait_recv()

    def sent(name, source, count, where=0):
        whole = source.at[pl.ds(0, count)]
        remote(whole, whole, name, where, {"section": 1 - sec}).wait_send()

    def load(source, target, n):
        return pltpu.make_async_copy(source, target, s["wsem"].at[n])

    load_qkv = load(wqkv_hbm, s["wqkv"], 0)
    load_raw = load(raw_hbm, s["raw"], 1)
    load_pack = load(pack_hbm, s["pack"], 2)
    load_far = load(far_hbm, s["far"], 3)
    load_wo = load(wo_hbm, s["wo"], 4)
    load_wd = load(wd_hbm, s["wd"], 5)
    load_qkv.start()

    @pl.when(sec == 0)
    def _():
        for h in range(n_half):
            load(tok_hbm.at[:, :, pl.ds(h * hcols, hcols)], xin.at[h], 6 + h).start()

    barrier = pltpu.get_barrier_semaphore()

    def greet_section():
        for k in ring + [0]:
            pl.semaphore_signal(barrier, inc=1, device_id={"section": 1 - sec, **head_peer(k)}, device_id_type=MESH)

    pl.when(sec == 1)(greet_section)
    for step in FAR_FIRST:
        pl.semaphore_signal(barrier, inc=1, device_id=req_peer(step), device_id_type=MESH)
    for k in ring:
        pl.semaphore_signal(barrier, inc=1, device_id=head_peer(k), device_id_type=MESH)
    pl.when(sec == 0)(greet_section)

    for other in (load_raw, load_pack, load_far, load_wo, load_wd):
        other.start()

    def lane_sum(mask, shape):
        lens = jnp.broadcast_to(len_ref[...].astype(F32), shape)
        return jnp.sum(jnp.where(mask, lens, 0.0), axis=1, keepdims=True)

    r16 = lax.broadcasted_iota(jnp.int32, (16, 16), 0)
    k16 = lax.broadcasted_iota(jnp.int32, (16, 16), 1)
    is_long = (lax.broadcasted_iota(jnp.int32, (16, 1), 0) == 0) & ((me == 0) | (me == mid))
    position = lane_sum(k16 == r16, (16, 16)) + jnp.where(is_long, float(LONG), 0.0)

    lanes = lax.broadcasted_iota(jnp.int32, (rows, HEAD), 1)
    lane16 = lax.broadcasted_iota(jnp.int32, (16, HEAD), 1)

    def normed(source, gain_ref):
        squares = jnp.zeros((rows, 1), F32)
        for h in range(n_half):
            at = pl.ds(h * hcols, hcols)
            x = source[h].reshape(rows, hcols).astype(F32)
            squares = squares + jnp.sum(x * x, axis=1, keepdims=True)
            s["xg"][:, at] = (x * gain_ref[:, at].astype(F32)).astype(BF16)
        return squares

    def first_products():
        squares = normed(xin, gain1_ref)
        load_qkv.wait()

        @pl.loop(0, ext_at // 256, unroll=True)
        def _(c):
            at = pl.ds(pl.multiple_of(c * 256, 256), 256)
            part = jnp.dot(s["xg"][...], s["wqkv"][:, at], preferred_element_type=F32)
            s["send1"][:, :, at] = part.astype(BF16).reshape(n_req, 16, 256)

        ext = s["ext"]
        for j in range(2):
            row = s["send1"][j * mid, :, 0:qw].astype(F32)[0:1]
            for h in range(HEADS):
                ext[j * 8 + h : j * 8 + h + 1, :] = row[:, h * HEAD : (h + 1) * HEAD]
        head = ext[...].astype(BF16)
        first = position[0:1]
        upper = jnp.floor(first * (1.0 / 256.0))
        lower = first - 256.0 * upper
        row16 = lax.broadcasted_iota(jnp.int32, (16, HEAD), 0)
        far_squares = jnp.where(row16 < 8, squares[0:1], squares[mid * 16 : mid * 16 + 1])
        far_high = far_squares.astype(BF16).astype(F32)
        common = jnp.where(
            lane16 < 80, far_high, jnp.where(lane16 < 96, far_squares - far_high, jnp.where(lane16 < 112, upper, lower))
        )
        high = squares.astype(BF16).astype(F32)
        pair = jnp.where(lanes < 32, high, squares - high).reshape(n_req, 16, HEAD)
        for g in range(n_req):
            s["send1"][g, :, ext_at : ext_at + HEAD] = head
            s["send1"][g, :, stat_at : stat_at + HEAD] = jnp.where(lane16 < 64, pair[g], common).astype(BF16)

    def split_gate():
        load_raw.wait()
        raw, wgu = s["raw"], s["wgu"]

        @pl.loop(0, cols // 16)
        def _(k):
            at = pl.ds(pl.multiple_of(k * 16, 16), 16)
            for c in range(ff // HEAD):
                source = pl.ds(c * HEAD, HEAD)
                wgu[at, pl.ds(c * 256, HEAD)] = raw[at, 0, source]
                wgu[at, pl.ds(c * 256 + HEAD, HEAD)] = raw[at, 1, source]

    @pl.when(sec == 0)
    def _():
        for h in range(n_half):
            load(tok_hbm.at[:, :, pl.ds(h * hcols, hcols)], xin.at[h], 6 + h).wait()
        first_products()

    pl.semaphore_wait(barrier, n_req - 1 + n_head - 1 + n_head)

    @pl.when(sec == 1)
    def _():
        split_gate()
        for h in range(n_half):
            remote(xin.at[h], xin.at[h], "in", h, {"section": 0}).wait_recv()
        remote(xin, s["out"], "back", 0, {"section": 0}).start()
        first_products()

    spread_req("p1", lambda p: s["send1"].at[p], s["recv1"])
    s["recv1"][me] = s["send1"][me]

    @pl.when(sec == 0)
    def _():
        split_gate()

    own_table = rope_tables(position, inv_ref[...])
    r_id = lax.broadcasted_iota(jnp.int32, (16 * HEADS, 16), 0) & 15
    k_id = lax.broadcasted_iota(jnp.int32, (16 * HEADS, 16), 1)
    seg_end = lane_sum(k_id <= r_id, (16 * HEADS, 16)).astype(jnp.int32)
    seg_start = lane_sum(k_id < r_id, (16 * HEADS, 16)).astype(jnp.int32)
    load_pack.wait()
    load_far.wait()
    pack, far = s["pack"], s["far"]
    recv1 = s["recv1"]
    arrived("p1", recv1, n_req - 1)

    def total_of(ref, at):
        value = ref[0, :, at].astype(F32)
        for p in range(1, ref.shape[0]):
            value = value + ref[p, :, at].astype(F32)
        return value

    stat = total_of(recv1, pl.ds(stat_at, HEAD))
    row_scale = lax.rsqrt((stat[:, 0:1] + stat[:, 32:33]) / width + EPSILON)

    for h in range(HEADS):
        at = pl.ds(h * HEAD, HEAD)
        s["q"][h] = rope(total_of(recv1, at) * row_scale, own_table).astype(BF16)

    new_key = rope(total_of(recv1, pl.ds(qw, HEAD)) * row_scale, own_table).astype(BF16)
    new_value = (total_of(recv1, pl.ds(qw + HEAD, HEAD)) * row_scale).astype(BF16)
    queries = s["q"][...].reshape(HEADS * 16, HEAD)
    keys = jnp.concatenate([new_key.astype(F32)] * HEADS, axis=0)
    values = jnp.concatenate([new_value.astype(F32)] * HEADS, axis=0)
    own = jnp.sum(queries.astype(F32) * keys, axis=1, keepdims=True) * scale

    total = total_of(recv1, pl.ds(ext_at, HEAD))
    far_scale = lax.rsqrt((stat[:, 64:65] + stat[:, 80:81]) / width + EPSILON)
    low8 = lax.broadcasted_iota(jnp.int32, (16, HEAD), 0) < 8
    places = jnp.where(
        low8, recv1[0, :, stat_at : stat_at + HEAD].astype(F32), recv1[mid, :, stat_at : stat_at + HEAD].astype(F32)
    )
    far_table = rope_tables(places[:, 96:97] * 256.0 + places[:, 112:113], inv_ref[...])
    far_query = rope(total * far_scale, far_table).astype(BF16)

    chunk = min(512, slots)
    n_chunk = slots // chunk
    contract = (((1,), (1,)), ((), ()))
    low_chunk = lax.broadcasted_iota(jnp.int32, (16, chunk), 0) < 8
    live = jnp.where(low_chunk, split_ref[0, 0], split_ref[0, 1])

    def scores_of(c, best):
        far_best, near_best = best
        at = pl.ds(pl.multiple_of(c * chunk, chunk), chunk)
        a = lax.dot_general(far_query, far[0, at, 0:HEAD], contract, preferred_element_type=F32)
        b = lax.dot_general(far_query, far[1, at, 0:HEAD], contract, preferred_element_type=F32)
        slot = lax.broadcasted_iota(jnp.int32, (16, chunk), 1) + c * chunk
        value = jnp.where(slot < live, jnp.where(low_chunk, a, b) * scale, NEG)
        s["fscore"][:, at] = value
        far_best = jnp.maximum(far_best, jnp.max(value, axis=1, keepdims=True))
        near = lax.dot_general(queries, pack[at, 0:HEAD], contract, preferred_element_type=F32)
        slot = lax.broadcasted_iota(jnp.int32, (HEADS * 16, chunk), 1) + c * chunk
        value = jnp.where((slot >= seg_start) & (slot < seg_end), near * scale, NEG)
        s["score"][:, at] = value
        return far_best, jnp.maximum(near_best, jnp.max(value, axis=1, keepdims=True))

    far_max, row_max = lax.fori_loop(0, n_chunk, scores_of, (jnp.full((16, 1), NEG, F32), own), unroll=True)
    own_weight = jnp.exp(own - row_max).astype(BF16).astype(F32)

    def sums_of(c, carry):
        far_totals, far_sum, totals, summed = carry
        at = pl.ds(pl.multiple_of(c * chunk, chunk), chunk)
        w = jnp.exp(s["fscore"][:, at] - far_max).astype(BF16)
        a = jnp.dot(w, far[0, at, HEAD:], preferred_element_type=F32)
        b = jnp.dot(w, far[1, at, HEAD:], preferred_element_type=F32)
        far_totals = far_totals + jnp.sum(w.astype(F32), axis=1, keepdims=True)
        far_sum = far_sum + jnp.where(low8, a, b)
        w = jnp.exp(s["score"][:, at] - row_max).astype(BF16)
        summed = summed + jnp.dot(w, pack[at, HEAD:], preferred_element_type=F32)
        return far_totals, far_sum, totals + jnp.sum(w.astype(F32), axis=1, keepdims=True), summed

    far_totals, far_sum, totals, summed = lax.fori_loop(
        0, n_chunk, sums_of,
        (jnp.zeros((16, 1), F32), jnp.zeros((16, HEAD), F32), own_weight, own_weight * values),
        unroll=True,
    )
    far_out = far_sum / far_totals
    far_lse = jnp.broadcast_to(far_max + jnp.log(far_totals), (16, HEAD))
    attended = summed / totals
    s["att"][...] = attended
    s["lse"][...] = jnp.broadcast_to(row_max + jnp.log(totals), (HEADS * 16, HEAD))
    mixed = s["mixed"]
    for h in range(HEADS):
        mixed[me, :, h * HEAD : (h + 1) * HEAD] = attended[h * 16 : (h + 1) * 16].astype(BF16)

    first_out = s["att"][pl.ds(0, HEADS, stride=16), :]
    first_lse = s["lse"][pl.ds(0, HEADS, stride=16), :]
    near_out = jnp.concatenate([first_out, first_out], axis=0)
    near_lse = jnp.concatenate([first_lse, first_lse], axis=0)
    owned = jnp.where(low8, 0, mid) == me
    peak = jnp.maximum(far_lse, near_lse)
    fa = jnp.exp(far_lse - peak)
    na = jnp.exp(near_lse - peak)
    part_out = jnp.where(owned, (fa * far_out + na * near_out) / (fa + na), far_out)
    part_lse = jnp.where(owned, peak + jnp.log(fa + na), far_lse)
    high = part_lse.astype(BF16).astype(F32)
    middle = (part_lse - high).astype(BF16).astype(F32)
    low = part_lse - high - middle
    mixed[me, :, qw : qw + HEAD] = part_out.astype(BF16)
    mixed[me, :, qw + HEAD :] = jnp.where(lane16 < 32, high, jnp.where(lane16 < 64, middle, low)).astype(BF16)
    spread_req("p2", lambda p: mixed.at[me], mixed)
    sent("p1", s["send1"], n_req - 1)
    load_wo.wait()
    arrived("p2", mixed, n_req - 1)

    parts = []
    for p in range(n_req):
        part = mixed[p, :, qw + HEAD :].astype(F32)
        parts.append(part[:, 0:1] + part[:, 32:33] + part[:, 64:65])
    peak = functools.reduce(jnp.maximum, parts)
    den = jnp.zeros((16, 1), F32)
    num = jnp.zeros((16, HEAD), F32)
    for p in range(n_req):
        w = jnp.exp(parts[p] - peak)
        den = den + w
        num = num + w * mixed[p, :, qw : qw + HEAD].astype(F32)
    long_out = num / den
    sent("p2", mixed, n_req - 1)
    first = lax.broadcasted_iota(jnp.int32, (16, qw), 0) == 0
    for j in range(2):
        flat = jnp.concatenate([long_out[j * 8 + h : j * 8 + h + 1] for h in range(HEADS)], axis=1)
        block = mixed[j * mid, :, 0:qw].astype(F32)
        mixed[j * mid, :, 0:qw] = jnp.where(first, jnp.broadcast_to(flat, (16, qw)), block).astype(BF16)

    send3, recv3, res = s["send3"], s["recv3"], s["res"]
    for h in range(n_half):
        part = jnp.dot(mixed[:, :, 0:qw].reshape(rows, qw), s["wo"][:, pl.ds(h * hcols, hcols)], preferred_element_type=F32)
        send3[h] = part.astype(BF16).reshape(n_head, blk, hcols)
        spread_head("p3", lambda p, h=h: send3.at[h, p], recv3.at[h], h)

    def block_total(buffer, mine, h):
        value = mine[h, mz].astype(F32)
        for k in range(1, n_head):
            value = value + buffer[h, lax.rem(mz + k, n_head)].astype(F32)
        return value

    for h in range(n_half):
        arrived("p3", recv3.at[h], n_head - 1, h)
        res[h, mz] = (xin[h, mz].astype(F32) + block_total(recv3, send3, h)).astype(BF16)
        spread_head("p4", lambda p, h=h: res.at[h, mz], res.at[h], h)
    for h in range(n_half):
        sent("p3", send3.at[h], n_head - 1, h)
    for h in range(n_half):
        arrived("p4", res.at[h], n_head - 1, h)

    squares = normed(res, gain2_ref)
    n_part = len(ff_parts)

    def along(side, k):
        if side == 0:
            c = lax.rem(mx + k, SIDE)
            return c, {"req": c * SIDE + my}
        c = lax.rem(my + k, SIDE)
        return c, {"req": mx * SIDE + c}

    coordinate = (mx, my)
    for g, (begin, end) in enumerate(ff_parts):
        buf = s[f"fs{g}"]

        @pl.loop(begin, end, unroll=True)
        def _(c, g=g, buf=buf, begin=begin):
            part = jnp.dot(
                s["xg"][...], s["wgu"][:, pl.ds(pl.multiple_of(c * 256, 256), 256)], preferred_element_type=F32
            ).astype(BF16).reshape(SIDE, SIDE, 16, 256)
            at = pl.ds(pl.multiple_of((c - begin) * 256, 256), 256)
            for a in range(SIDE):
                if g % 2 == 0:
                    buf[a, :, :, at] = part[a]
                else:
                    buf[a, :, :, at] = part[:, a]

        if g == 0:
            at = pl.ds((end - begin) * 256, HEAD)
            buf[:, :, :, at] = split_two(squares, lanes).reshape(SIDE, SIDE, 16, HEAD)
        for k in (2, 1, 3):
            c, peer = along(g % 2, k)
            remote(buf.at[c], s[f"fr{g}"].at[coordinate[g % 2]], "f1", g, peer).start()
    for h in range(n_half):
        sent("p4", res.at[h], n_head - 1, h)

    for g, (begin, end) in enumerate(ff_parts):
        side = g % 2
        buf, got, turn = s[f"fs{g}"], s[f"fr{g}"], s[f"ft{g}"]
        arrived("f1", got, SIDE - 1, g)
        mine = coordinate[side]

        @pl.loop(0, SIDE, unroll=True)
        def _(b, g=g, buf=buf, got=got, turn=turn, mine=mine, begin=begin, end=end):
            value = buf[mine, b].astype(F32)
            for k in range(1, SIDE):
                value = value + got[lax.rem(mine + k, SIDE), b].astype(F32)
            turn[b] = value.astype(BF16)
            if g == 0:
                stat = value[:, (end - begin) * 256 :]
                turn[b, :, pl.ds((end - begin) * 256, HEAD)] = split_two(stat[:, 0:1] + stat[:, 64:65], lane16)

        for k in (2, 1, 3):
            c, peer = along(1 - side, k)
            remote(turn.at[c], s[f"fu{g}"].at[coordinate[1 - side]], "f2", g, peer).start()

    ff_scale = None
    hid = [s[f"hid{w}"] for w in range(len(SETS))]
    for g, (begin, end) in enumerate(ff_parts):
        side = g % 2
        turn, got = s[f"ft{g}"], s[f"fu{g}"]
        arrived("f2", got, SIDE - 1, g)
        mine = coordinate[1 - side]

        def turned(at, turn=turn, got=got, mine=mine):
            value = turn[mine, :, at].astype(F32)
            for k in range(1, SIDE):
                value = value + got[lax.rem(mine + k, SIDE), :, at].astype(F32)
            return value

        if g == 0:
            stat = turned(pl.ds((end - begin) * 256, HEAD))
            ff_scale = lax.rsqrt((stat[:, 0:1] + stat[:, 64:65]) / width + EPSILON)
        which = next(w for w, members in enumerate(SETS) if g in members)
        base = ff_parts[SETS[which][0]][0]
        for c in range(begin, end):
            both = turned(pl.ds((c - begin) * 256, 256)) * ff_scale
            gate, up = both[:, :HEAD], both[:, HEAD:]
            hid[which][me, :, pl.ds((c - base) * HEAD, HEAD)] = (gate / (1.0 + jnp.exp(-gate)) * up).astype(BF16)
        if g == SETS[which][-1]:
            spread_req("p6", lambda p, which=which: hid[which].at[me], hid[which], which)
    for g in range(n_part):
        sent("f1", s[f"fs{g}"], SIDE - 1, g)
        sent("f2", s[f"ft{g}"], SIDE - 1, g)

    load_wd.wait()
    send7, recv7, oblk, out, down = s["send7"], s["recv7"], s["oblk"], s["out"], s["down"]
    done = 0
    for which, wide in enumerate(wides):
        arrived("p6", hid[which], n_req - 1, which)
        for h in range(n_half):
            at = pl.ds(h * hcols, hcols)
            part = jnp.dot(
                hid[which][...].reshape(rows, wide), s["wd"][pl.ds(done, wide), at], preferred_element_type=F32
            )
            if which > 0:
                part = down[:, at] + part
            if which < len(SETS) - 1:
                down[:, at] = part
            else:
                send7[h] = part.astype(BF16).reshape(n_head, blk, hcols)
                spread_head("p7", lambda p, h=h: send7.at[h, p], recv7.at[h], h)
        done += wide
    for which in range(len(SETS)):
        sent("p6", hid[which], n_req - 1, which)

    def hand_over(k, h):
        return remote(oblk.at[h], xin.at[h, mz], "in", h, {"section": 1, **head_peer(k)})

    for h in range(n_half):
        arrived("p7", recv7.at[h], n_head - 1, h)
        oblk[h] = (res[h, mz].astype(F32) + block_total(recv7, send7, h)).astype(BF16)

        @pl.when(sec == 0)
        def _(h=h):
            for k in ring + [0]:
                hand_over(k, h).start()

        @pl.when(sec == 1)
        def _(h=h):
            out[h, mz] = oblk[h]
            spread_head("p8", lambda p: oblk.at[h], out.at[h], h)

    for h in range(n_half):
        sent("p7", send7.at[h], n_head - 1, h)

    @pl.when(sec == 0)
    def _():
        remote(xin, out, "back", 0, {"section": 1}).wait_recv()
        for h in range(n_half):
            remote(xin.at[h], xin.at[h], "in", h, {"section": 1}).wait_send()

    @pl.when(sec == 1)
    def _():
        for h in range(n_half):
            arrived("p8", out.at[h], n_head - 1, h)
            out_ref[:, :, pl.ds(h * hcols, hcols)] = out[h]

    @pl.when(sec == 0)
    def _():
        for h in range(n_half):
            out_ref[:, :, pl.ds(h * hcols, hcols)] = out[h]

    @pl.when(sec == 1)
    def _():
        for h in range(n_half):
            sent("p8", out.at[h], n_head - 1, h)
        remote(xin, out, "back", 0, {"section": 0}).wait_send()


def local(
    tokens,
    attention_gain,
    query_key_value_weight,
    head_output_weight,
    feedforward_gain,
    gate_up,
    down_weight,
    packed_cache,
    long_cache,
    lengths,
    long_split,
):
    n_req = lax.axis_size("req")
    n_head = lax.axis_size("head")
    rows, cols = tokens.shape
    blk = rows // n_head
    qkv = query_key_value_weight.shape[3]
    qw = head_output_weight.shape[2]
    ff = down_weight.shape[1]
    slots = packed_cache.shape[1]
    assert slots == long_cache.shape[2] and rows == n_req * 16 and n_req == SIDE * SIDE
    half = (PIECES, n_head, blk, cols // PIECES)
    n = ff // HEAD
    cuts = [sum(PARTS[:g]) * n // sum(PARTS) for g in range(len(PARTS) + 1)]
    ff_parts = tuple(zip(cuts[:-1], cuts[1:]))
    wides = [(ff_parts[members[-1]][1] - ff_parts[members[0]][0]) * HEAD for members in SETS]
    freq_ids = np.arange(HEAD // 2, dtype=np.float32)
    inverse = np.float32(1.0) / np.power(np.float32(10000.0), freq_ids * np.float32(2.0) / np.float32(HEAD))
    inverse = jnp.asarray(np.concatenate([inverse, inverse])[None].astype(np.float32))
    vmem = pl.BlockSpec(memory_space=pltpu.VMEM)
    hbm = pl.BlockSpec(memory_space=pl.ANY)
    smem = pl.BlockSpec(memory_space=pltpu.SMEM)
    scratch = dict(
        wqkv=pltpu.VMEM((cols, qkv), BF16),
        wo=pltpu.VMEM((qw, cols), BF16),
        raw=pltpu.VMEM((cols, 2, ff), BF16),
        wgu=pltpu.VMEM((cols, 2 * ff), BF16),
        wd=pltpu.VMEM((ff, cols), BF16),
        pack=pltpu.VMEM((slots, 2 * HEAD), BF16),
        far=pltpu.VMEM((2, slots, 2 * HEAD), BF16),
        xin=pltpu.VMEM(half, BF16),
        xg=pltpu.VMEM((rows, cols), BF16),
        send1=pltpu.VMEM((n_req, 16, qkv + 2 * HEAD), BF16),
        recv1=pltpu.VMEM((n_req, 16, qkv + 2 * HEAD), BF16),
        ext=pltpu.VMEM((16, HEAD), F32),
        q=pltpu.VMEM((HEADS, 16, HEAD), BF16),
        score=pltpu.VMEM((HEADS * 16, slots), F32),
        fscore=pltpu.VMEM((16, slots), F32),
        att=pltpu.VMEM((HEADS * 16, HEAD), F32),
        lse=pltpu.VMEM((HEADS * 16, HEAD), F32),
        mixed=pltpu.VMEM((n_req, 16, qw + 2 * HEAD), BF16),
        send3=pltpu.VMEM(half, BF16),
        recv3=pltpu.VMEM(half, BF16),
        res=pltpu.VMEM(half, BF16),
        down=pltpu.VMEM((rows, cols), F32),
        send7=pltpu.VMEM(half, BF16),
        recv7=pltpu.VMEM(half, BF16),
        oblk=pltpu.VMEM((PIECES, blk, cols // PIECES), BF16),
        out=pltpu.VMEM(half, BF16),
        wsem=pltpu.SemaphoreType.DMA((6 + PIECES,)),
    )
    for w, wide in enumerate(wides):
        scratch[f"hid{w}"] = pltpu.VMEM((n_req, 16, wide), BF16)
    for g, (begin, end) in enumerate(ff_parts):
        wide = (end - begin) * 256 + (HEAD if g == 0 else 0)
        scratch[f"fs{g}"] = pltpu.VMEM((SIDE, SIDE, 16, wide), BF16)
        scratch[f"fr{g}"] = pltpu.VMEM((SIDE, SIDE, 16, wide), BF16)
        scratch[f"ft{g}"] = pltpu.VMEM((SIDE, 16, wide), BF16)
        scratch[f"fu{g}"] = pltpu.VMEM((SIDE, 16, wide), BF16)
    for name, count in dict(
        p1=1, p2=1, p3=PIECES, p4=PIECES, f1=len(PARTS), f2=len(PARTS), p6=len(SETS), p7=PIECES, p8=PIECES,
        **{"in": PIECES}, back=1,
    ).items():
        scratch["ss_" + name] = pltpu.SemaphoreType.DMA((count,))
        scratch["rs_" + name] = pltpu.SemaphoreType.DMA((count,))
    names = list(scratch)

    def body(*refs):
        plain, rest = refs[:13], refs[13:]
        kernel((n_req, n_head, cols * n_req), ff_parts, wides, *plain, dict(zip(names, rest)))

    out = pl.pallas_call(
        body,
        out_shape=pltpu.VMEM((n_head, blk, cols), BF16),
        in_specs=[smem, hbm, vmem, hbm, hbm, vmem, hbm, hbm, hbm, hbm, vmem, vmem],
        out_specs=vmem,
        scratch_shapes=[scratch[name] for name in names],
        compiler_params=pltpu.CompilerParams(
            collective_id=0, has_side_effects=True, vmem_limit_bytes=56 * 2**20
        ),
        name="two_layers",
    )(
        long_split.T,
        tokens.reshape(n_head, blk, cols),
        attention_gain,
        query_key_value_weight.reshape(cols, qkv),
        head_output_weight.reshape(qw, cols),
        feedforward_gain,
        gate_up.reshape(cols, 2, ff),
        down_weight.reshape(ff, cols),
        packed_cache.reshape(slots, 2 * HEAD),
        long_cache.reshape(2, slots, 2 * HEAD),
        lengths,
        inverse,
    )
    return out.reshape(1, rows, cols)


def solution(mesh):
    placed = (
        P(None, "req"),
        P("section", "req"),
        P("section", "req", "head", None),
        P("section", "head", None, "req"),
        P("section", "req"),
        P("section", "req", None, "head"),
        P("section", "head", "req"),
        P("section", "req", "head", None),
        P("section", None, "req", "head", None),
        P("req", None),
        P(None, "req"),
    )
    return jax.shard_map(
        local, mesh=mesh, in_specs=placed, out_specs=P("section", None, "req"), check_vma=False
    )
```
